512 devices in a mesh: tm: 8 (over y, core), freq: 16 (over z), dish: 4 (over x).
Axes of the slice: x: 4, y: 4, z: 16, core: 2. Of those that a mesh axis runs over, the one named last changes fastest.
Arguments:
- time_data: bfloat16 [64, 512, 4096], P('dish', 'freq', 'tm'), may hold values from -24 to 24
- pointing: bfloat16 [32, 128, 128], P('tm'), may hold values from -0.5 to 0.5
- coverage: int32 [32], P('tm'), may hold values from 0 to 15
- noise_inv: bfloat16 [64, 128, 128], P('dish'), as said below
- gains: float32 [64, 512, 32], P('dish', 'freq', 'tm'), may hold values from 0.1 to 1.9
- prior_inv: float32 [512, 512], replicated, as said below
- precond: float32 [512, 8192], P('freq', ('tm', 'dish')), may hold values from 0.5 to 200
Outputs:
- map_estimate: float32 [512, 8192], P('freq', ('tm', 'dish'))
- residual: float32 [512, 8192], P('freq', ('tm', 'dish'))
The draws below stay inside these ranges and needn't reach their ends.
Inputs may be any that keep to these rules, and one draw needn't show every extreme that they name: `noise_inv`: each matrix is symmetric with a positive diagonal that dominates its row, and zero where two samples lie more than 16 apart. `prior_inv`: symmetric with a positive diagonal that dominates its row.
All inputs are finite; a program needn't handle non-finite values.
Results may differ from the reference program's by a relative error of at most 0.0045.
Values may be sent and summed in bfloat16 or wider, within the bound.
No kernel may reach another device: no remote copies, remote signals or barrier semaphores. Data moves between devices by JAX's collectives and lax.ppermute only.
A program may use at most 64 MiB of HBM per device.

```python
import math
import jax
import jax.numpy as jnp
from jax import lax

CHANNELS = 512
BLK_DEV = 4
BAND = 16
ITERS = 4
DISHES = 64
BLOCKS = 32
SAMPLES = 4096
REG = 8
TILES = 64
NPIX = 8192


def draw_coverage(key, part):
    subkeys = jax.random.split(key, 5)
    spans = BLOCKS // BLK_DEV
    block_index = jnp.arange(BLOCKS, dtype=jnp.int32)
    span_index = block_index // BLK_DEV
    position = block_index % BLK_DEV
    spread_values = jax.random.randint(subkeys[0], (BLOCKS,), 0, 2 * REG)
    hot_values = jax.random.randint(subkeys[1], (spans,), 0, 2 * REG)
    picked = jax.random.randint(subkeys[2], (BLOCKS,), 0, 2)
    own_values = jax.random.randint(subkeys[3], (BLOCKS,), 0, REG)
    next_values = jax.random.randint(subkeys[4], (BLOCKS,), REG, 2 * REG)
    values = jnp.where(picked == 1, hot_values[span_index], spread_values)
    values = jnp.where(position == 0, own_values, values)
    values = jnp.where(position == 1, next_values, values)
    values = jnp.where(block_index == 0, 0, values)
    values = jnp.where(block_index == 1, 2 * REG - 1, values)
    return values.astype(jnp.int32)


def draw_noise_inv(key, part):
    subkeys = jax.random.split(key, 3)
    raw_values = jax.random.uniform(subkeys[0], (DISHES, 128, 128), jnp.float32, -1.0, 1.0)
    symmetric = 0.5 * (raw_values + jnp.swapaxes(raw_values, 1, 2))
    samples = jnp.arange(128, dtype=jnp.int32)
    distance = jnp.abs(samples[:, None] - samples[None, :])
    inside = (distance <= BAND) & (distance > 0)
    noise_level = jax.random.uniform(subkeys[1], (DISHES, 1, 1), jnp.float32, 0.5, 2.0)
    diagonal = 1.0 + 0.5 * jax.random.uniform(subkeys[2], (DISHES, 128, 1), jnp.float32)
    matrix = jnp.where(inside, symmetric / (2.5 * BAND), 0.0) + jnp.where(distance == 0, diagonal, 0.0)
    return (noise_level / DISHES * matrix).astype(jnp.bfloat16)


def draw_prior_inv(key, part):
    subkeys = jax.random.split(key, 2)
    raw_values = jax.random.uniform(subkeys[0], (CHANNELS, CHANNELS), jnp.float32, -1.0, 1.0)
    symmetric = 0.5 * (raw_values + raw_values.T)
    channel_ids = jnp.arange(CHANNELS, dtype=jnp.int32)
    apart = channel_ids[:, None] != channel_ids[None, :]
    diagonal = 3.5 + 2.0 * jax.random.uniform(subkeys[1], (CHANNELS, 1), jnp.float32)
    return jnp.where(apart, symmetric * (3.0 / CHANNELS), 0.0) + jnp.where(apart, 0.0, diagonal)


def draw_precond(key, part):
    col_level = jnp.arange(NPIX, dtype=jnp.float32)[None, :] / NPIX
    row_level = jnp.arange(CHANNELS, dtype=jnp.float32)[:, None] / CHANNELS
    base_values = jnp.exp(jax.random.uniform(key, (CHANNELS, NPIX), jnp.float32, math.log(0.5), math.log(2.0)))
    return base_values * jnp.power(10.0, col_level) * jnp.power(10.0, row_level)


def steps_of(stream_key, extent, cuts, low, high):
    loudness, own = 1.0, jax.random.fold_in(stream_key, 6)
    for dim, parts in cuts:
        steps = jnp.exp(jax.random.uniform(jax.random.fold_in(own, dim), (parts,), jnp.float32, low / len(cuts), high / len(cuts)))
        loudness = loudness * jnp.repeat(steps, extent[dim] // parts).reshape([-1 if axis == dim else 1 for axis in range(len(extent))])
    return loudness


def centred(stream_key, dims, width, limit, cuts=(), kind=jnp.bfloat16):
    factor_of = steps_of(stream_key, dims, cuts, -0.22, 0.18) if cuts else 1.0
    array = jax.random.normal(stream_key, dims, jnp.float32) * width * factor_of
    return jnp.minimum(jnp.maximum(array, -limit), limit).astype(kind)


def setup_inputs(seed: int = 0) -> dict:
    key_of = jax.random.split(jax.random.key(seed), 8)
    time_data = centred(key_of[0], (DISHES, CHANNELS, SAMPLES), 4.0, 24.0, ((0, 4), (1, 16), (2, 8)))
    pointing = centred(key_of[1], (BLOCKS, 128, 128), 128 ** -0.5, 0.5, ((0, 8),))
    coverage = draw_coverage(jax.random.fold_in(key_of[7], 71), 0)
    noise_inv = draw_noise_inv(jax.random.fold_in(key_of[7], 71), 0)
    gains = jnp.clip(1.0 + 0.18 * jax.random.normal(key_of[4], (DISHES, CHANNELS, BLOCKS), jnp.float32), 0.1, 1.9)
    prior_inv = draw_prior_inv(jax.random.fold_in(key_of[7], 71), 0)
    precond = draw_precond(jax.random.fold_in(key_of[7], 71), 0)
    return {"time_data": time_data, "pointing": pointing, "coverage": coverage, "noise_inv": noise_inv, "gains": gains, "prior_inv": prior_inv, "precond": precond}


def reference(time_data, pointing, coverage, noise_inv, gains, prior_inv, precond):
    highest = lax.Precision.HIGHEST
    scan_index = jnp.arange(BLOCKS, dtype=jnp.int32) // BLK_DEV
    tile_of = ((scan_index * REG + coverage) % TILES).astype(jnp.int32)
    point_wide = pointing.astype(jnp.float32)

    def back_project(weighted):
        rounded = lax.optimization_barrier(weighted.astype(jnp.bfloat16)).astype(jnp.float32)
        tile_part = jnp.einsum("cbt,bti->cbi", rounded, point_wide, precision=highest)
        summed = jnp.zeros((CHANNELS, TILES, 128), jnp.float32).at[:, tile_of, :].add(tile_part)
        return summed.reshape(CHANNELS, NPIX)

    def data_term(map_field):
        rounded = lax.optimization_barrier(map_field.astype(jnp.bfloat16)).astype(jnp.float32)
        tile_maps = rounded.reshape(CHANNELS, TILES, 128)[:, tile_of, :]
        model_tod = jnp.einsum("cbp,bsp->cbs", tile_maps, point_wide, precision=highest)
        model_tod = lax.optimization_barrier(model_tod.astype(jnp.bfloat16)).astype(jnp.float32)

        def dish_step(running, dish_items):
            weight, matrix = dish_items
            dish_term = jnp.einsum("cbs,st->cbt", model_tod, matrix.astype(jnp.float32), precision=highest)
            return running + (weight * weight)[:, :, None] * dish_term, None

        mixed_tod, unused = lax.scan(dish_step, jnp.zeros((CHANNELS, BLOCKS, 128), jnp.float32), (gains, noise_inv))
        return back_project(mixed_tod)

    def operate(map_field):
        return data_term(map_field) + jnp.dot(prior_inv, map_field, precision=highest)

    def rhs_step(running, dish_items):
        weight, matrix, series = dish_items
        blocked = series.astype(jnp.float32).reshape(CHANNELS, BLOCKS, 128)
        dish_term = jnp.einsum("cbs,st->cbt", blocked, matrix.astype(jnp.float32), precision=highest)
        return running + weight[:, :, None] * dish_term, None

    rhs_tod, unused = lax.scan(rhs_step, jnp.zeros((CHANNELS, BLOCKS, 128), jnp.float32), (gains, noise_inv, time_data))
    right_side = back_project(rhs_tod)
    estimate = jnp.zeros_like(right_side)
    residual = right_side
    scaled = precond * residual
    direction = scaled
    energy_now = jnp.sum(residual * scaled)
    for iteration in range(ITERS):
        operated = operate(direction)
        step_size = energy_now / jnp.sum(direction * operated)
        estimate = estimate + step_size * direction
        residual = residual - step_size * operated
        if iteration + 1 < ITERS:
            scaled = precond * residual
            energy_next = jnp.sum(residual * scaled)
            direction = scaled + (energy_next / energy_now) * direction
            energy_now = energy_next
    return estimate, residual
```

```python
import jax
import jax.numpy as jnp
from jax import lax
from jax.experimental import pallas as pl
from jax.experimental.pallas import tpu as pltpu
from jax.sharding import PartitionSpec as P

ITERS = 4
SENT = 254
CODES = 16383.0 / 0.9
DIAGS = 17
F32 = jnp.float32
BF16 = jnp.bfloat16
VMEM = pl.BlockSpec(memory_space=pltpu.VMEM)
SMEM = pl.BlockSpec(memory_space=pltpu.SMEM)


def split(x):
    high = x.astype(BF16)
    return high, (x - high.astype(F32)).astype(BF16)


def encode(gain):
    level = (gain - 1.0) * CODES
    count = jnp.floor(jnp.abs(level) + 0.5)
    place = jnp.floor(count * (1.0 / 128.0))
    value = 1.0 + (count - place * 128.0) * (1.0 / 128.0)
    value = value * 2.0 ** -63
    for step in (64, 32, 16, 8, 4, 2, 1):
        take = place >= step
        value = jnp.where(take, value * 2.0 ** step, value)
        place = jnp.where(take, place - step, place)
    return jnp.where(level < 0.0, -value, value)


def decode(code):
    value = jnp.abs(code)
    count = jnp.zeros_like(code)
    for step in (64, 32, 16, 8, 4, 2, 1):
        take = value >= 2.0 ** (step - 63)
        value = jnp.where(take, value * 2.0 ** -step, value)
        count = jnp.where(take, count + 128.0 * step, count)
    count = (count + (value * 2.0 ** 63 - 1.0) * 128.0) * (1.0 / CODES)
    return jnp.where(code < 0.0, 1.0 - count, 1.0 + count)


def dot_nt(a, b):
    return lax.dot_general(a, b, (((1,), (1,)), ((), ())), preferred_element_type=F32)


def prepare_kernel(data_ref, noise_ref, gain_ref, out_ref, band_ref):
    first_dish = lax.axis_index("dish") * 16
    lane = lax.broadcasted_iota(jnp.int32, (32, 128), 1)
    rows = lax.broadcasted_iota(jnp.int32, (32, 128), 0)
    pick = (lane == 127 - rows).astype(F32).astype(BF16)
    wide = lax.broadcasted_iota(jnp.int32, (128, 128), 1)
    tall = lax.broadcasted_iota(jnp.int32, (128, 128), 0)
    flip = (wide + tall == 127).astype(F32).astype(BF16)
    turned = [jnp.transpose(gain_ref[d]) for d in range(16)]
    rhs = [jnp.zeros((32, 128), F32) for _ in range(4)]
    squares = [jnp.zeros((32, 128), F32) for _ in range(2)]
    for d in range(16):
        noise = noise_ref[d]
        flipped = jnp.dot(noise, flip, preferred_element_type=F32)
        skewed = pltpu.roll(flipped, 0, 1, stride=1, stride_axis=0)
        band_ref[d * 32:(d + 1) * 32, :] = dot_nt(pick, skewed.astype(BF16))
        series = jnp.concatenate([data_ref[d, :, b * 128:(b + 1) * 128] for b in range(4)], axis=0)
        weighted = jnp.dot(series, noise, preferred_element_type=F32)
        for b in range(4):
            gain = jnp.broadcast_to(turned[d][:, b:b + 1], (32, 128))
            rhs[b] = rhs[b] + gain * weighted[b * 32:(b + 1) * 32]
            slot = (b % 2) * 64 + d + first_dish
            squares[b // 2] = jnp.where(lane == slot, gain, squares[b // 2])
    for k in range(DIAGS):
        out_ref[k * 16:(k + 1) * 16, :] = band_ref[pl.ds(k, 16, stride=32), :].astype(BF16)
    for b in range(4):
        high, low = split(rhs[b])
        out_ref[272 + b * 32:304 + b * 32, :] = high
        out_ref[400 + b * 32:432 + b * 32, :] = low
    for h in range(2):
        held = (lane & 63) - first_dish
        held = jnp.logical_and(held >= 0, held < 16)
        out_ref[528 + h * 32:560 + h * 32, :] = jnp.where(held, encode(squares[h]), 0.0).astype(BF16)


def project_kernel(cover_ref, gathered_ref, point_ref, own_ref, square_ref, ahead_ref):
    own = [jnp.zeros((32, 128), F32) for _ in range(2)]
    ahead = [jnp.zeros((32, 128), F32) for _ in range(2)]
    first_tile = lax.axis_index("dish") * 2
    lane = lax.broadcasted_iota(jnp.int32, (16, 128), 1)
    cover_row = jnp.zeros((16, 128), F32)
    for b in range(4):
        total = jnp.zeros((32, 128), F32)
        for j in range(4):
            total = total + gathered_ref[j, 272 + b * 32:304 + b * 32, :].astype(F32)
            total = total + gathered_ref[j, 400 + b * 32:432 + b * 32, :].astype(F32)
        part = jnp.dot(total.astype(BF16), point_ref[b], preferred_element_type=F32)
        tile = cover_ref[b]
        for t in range(2):
            own[t] = own[t] + jnp.where(tile == first_tile + t, part, 0.0)
            ahead[t] = ahead[t] + jnp.where(tile == first_tile + t + 8, part, 0.0)
        cover_row = jnp.where(lane == b, tile.astype(F32), cover_row)
        ahead_ref[192 + b * 128:320 + b * 128, :] = point_ref[b]
    square = jnp.zeros((64, 128), F32)
    for j in range(4):
        square = square + gathered_ref[j, 528:592, :].astype(F32)
    square_ref[...] = square.astype(BF16)
    ahead_ref[128:192, :] = square.astype(BF16)
    for t in range(2):
        own_ref[t * 32:(t + 1) * 32, :] = own[t]
        high, low = split(ahead[t])
        ahead_ref[t * 32:(t + 1) * 32, :] = high
        ahead_ref[64 + t * 32:96 + t * 32, :] = low
    ahead_ref[704:720, :] = cover_row.astype(BF16)


def start_kernel(own_ref, square_ref, arrived_ref, scale_ref, right_ref, out_ref):
    out_ref[64:128, :] = square_ref[...]
    out_ref[128:192, :] = arrived_ref[128:192, :]
    for t in range(2):
        rows = slice(t * 32, (t + 1) * 32)
        cols = slice(t * 128, (t + 1) * 128)
        right = (own_ref[rows, :] + arrived_ref[rows, :].astype(F32)
                 + arrived_ref[64 + t * 32:96 + t * 32, :].astype(F32))
        right_ref[:, cols] = right
        high, low = split(scale_ref[:, cols] * right)
        out_ref[rows, :] = high
        kept = SENT - 192 - t * 32 if t == 1 else 32
        out_ref[192 + t * 32:192 + t * 32 + kept, :] = low[:kept]


def unit(size):
    wide = lax.broadcasted_iota(jnp.int32, (size, size), 1)
    tall = lax.broadcasted_iota(jnp.int32, (size, size), 0)
    return (wide == tall).astype(F32).astype(BF16)


def woven():
    wide = lax.broadcasted_iota(jnp.int32, (128, 128), 1)
    tall = lax.broadcasted_iota(jnp.int32, (128, 128), 0)
    return (wide == (tall & 7) * 16 + (tall >> 3)).astype(F32).astype(BF16)


def weave_point(point, points, points_t, b):
    turn = woven()
    forward = jnp.dot(turn, point, preferred_element_type=F32).astype(BF16)
    flipped = dot_nt(unit(128), forward).astype(BF16)
    for half in range(2):
        points[b, :, half * 128:half * 128 + 128] = forward
        points_t[b, :, half * 128:half * 128 + 128] = flipped


def setup_kernel(noise_ref, prior_ref, point_ref, prior_cat, bands, points, points_t, factor_ref):
    turn = woven()
    prior = prior_ref[...]
    high, low = split(prior)
    prior_cat[0:512, :] = high
    prior_cat[512:1024, :] = low
    prior_cat[1024:1536, :] = high
    for k in range(DIAGS):
        piece = jnp.concatenate([noise_ref[j, k * 16:(k + 1) * 16, :] for j in range(4)] * 2, axis=0)
        bands[k * 128:(k + 1) * 128, :] = dot_nt(turn, piece).astype(BF16)
    for b in range(4):
        weave_point(point_ref[b], points, points_t, b)
    top = jnp.max(jnp.max(jnp.abs(prior), axis=0, keepdims=True), axis=1, keepdims=True)
    diag = jnp.zeros((16, 128), F32)
    for j in range(4):
        diag = diag + noise_ref[j, 0:16, :].astype(F32)
    level = jnp.sum(jnp.sum(diag, axis=0, keepdims=True), axis=1, keepdims=True) * (1.0 / 128.0)
    factor_ref[...] = jnp.broadcast_to(1.0 / (512.0 * (top + level)), (8, 128))


def choose_own():
    lane = lax.broadcasted_iota(jnp.int32, (32, 512), 1)
    line = lax.broadcasted_iota(jnp.int32, (32, 512), 0)
    return (lane == line + lax.axis_index("freq") * 32).astype(F32).astype(BF16)


def build_mixer(covers, bands, squares, mixer):
    first_tile = lax.axis_index("dish") * 2

    @pl.loop(0, 8)
    def _(b):
        cover = covers[b] - first_tile

        @pl.when(jnp.logical_and(cover >= 0, cover < 2))
        def _():
            square = squares[b]
            for k in range(DIAGS):
                mixer[b, k] = jnp.dot(bands[k * 128:(k + 1) * 128, :], square, preferred_element_type=F32)


def apply_mixer(b, mixer, model, mixed):
    @pl.loop(0, 4)
    def _(group):
        cols = pl.ds(pl.multiple_of(group * 128, 128), 128)
        near, sums = {}, {}

        def at(i):
            if i not in near:
                value = model[(i % 16) * 8:(i % 16) * 8 + 8, cols]
                near[i] = pltpu.roll(value, 7, 0) if i >= 16 else value
            return near[i]

        for i in range(16):
            own = at(i)
            weight = mixer[b, 0, i * 8:(i + 1) * 8, cols]
            total = weight * own
            if i in sums:
                total = total + sums[i]
            for k in range(1, DIAGS):
                weight = mixer[b, k, i * 8:(i + 1) * 8, cols]
                total = total + weight * at(i + k)
                spill = weight * own
                sums[i + k] = sums[i + k] + spill if i + k in sums else spill
            mixed[i * 8:(i + 1) * 8, cols] = total
        for i in range(16):
            mixed[i * 8:(i + 1) * 8, cols] += pltpu.roll(sums[16 + i], 1, 0)


def square_form(b, mixer, model):
    def step(group, running):
        cols = pl.ds(pl.multiple_of(group * 128, 128), 128)
        near = {}

        def at(i):
            if i not in near:
                value = model[(i % 16) * 8:(i % 16) * 8 + 8, cols]
                near[i] = pltpu.roll(value, 7, 0) if i >= 16 else value
            return near[i]

        for i in range(16):
            own = at(i)
            value = mixer[b, 1, i * 8:(i + 1) * 8, cols] * at(i + 1)
            for k in range(2, DIAGS):
                value = value + mixer[b, k, i * 8:(i + 1) * 8, cols] * at(i + k)
            value = 2.0 * value + mixer[b, 0, i * 8:(i + 1) * 8, cols] * own
            running = running + value * own
        return running

    return lax.fori_loop(0, 4, step, jnp.zeros((8, 128), F32))


def krylov_kernel(cover_ref, bands, gathered_ref, scales_ref, prior_cat, point_ref, flip_ref, factor_ref, arrived_ref,
                  moment_ref, covers, scale, squares, points, points_t, start_ref,
                  mixer, vector_cat, vector_stack, vector, image, scale_rows,
                  stage, stage_low, model, mixed, mixed_stack, forms):
    first_tile = lax.axis_index("dish") * 2
    eye = unit(128)
    for q in range(4):
        for f in range(16):
            stage[f * 32:(f + 1) * 32, :] = gathered_ref[f, 64 + q * 32:96 + q * 32, :]
        gain = decode(stage[...].astype(F32))
        high, low = split(gain * gain)
        high, low = dot_nt(eye, high).astype(BF16), dot_nt(eye, low).astype(BF16)
        for side in range(2):
            squares[2 * q + side, 0:64, :] = high[side * 64:side * 64 + 64]
            squares[2 * q + side, 64:128, :] = low[side * 64:side * 64 + 64]
    stage_low[...] = jnp.zeros_like(stage_low)
    for t in range(2):
        kept = SENT - 192 - t * 32 if t == 1 else 32
        if t == 1:
            stage_low[...] = jnp.zeros_like(stage_low)
        for f in range(16):
            stage[f * 32:(f + 1) * 32, :] = gathered_ref[f, t * 32:(t + 1) * 32, :]
            stage_low[f * 32:f * 32 + kept, :] = gathered_ref[f, 192 + t * 32:192 + t * 32 + kept, :]
        vector[t * 128:(t + 1) * 128, :] = dot_nt(eye, stage[...]) + dot_nt(eye, stage_low[...])
    start_ref[...] = vector[...]
    for f in range(16):
        scale_rows[f * 32:(f + 1) * 32, :] = scales_ref[f, 0:32, :]
    scale[...] = jnp.transpose(scale_rows[...])
    row = arrived_ref[704:720, :].astype(F32)[0:1, :]
    spot = lax.broadcasted_iota(jnp.int32, (1, 128), 1)
    for b in range(4):
        covers[b] = cover_ref[b]
        covers[4 + b] = jnp.sum(jnp.where(spot == b, row, 0.0)).astype(jnp.int32) - 8
        points[b] = point_ref[b]
        points_t[b] = flip_ref[b]
        weave_point(arrived_ref[192 + b * 128:320 + b * 128, :], points, points_t, 4 + b)
    factor = factor_ref[0:1, 0:1]
    build_mixer(covers, bands, squares, mixer)

    def total(a, b):
        both = a * b
        both = both[:, 0:128] + both[:, 128:256] + (both[:, 256:384] + both[:, 384:512])
        return jnp.sum(both, axis=0, keepdims=True)

    forms[...] = jnp.zeros_like(forms)
    sums = [total(vector[...] * vector[...], 1.0 / scale[...])]
    for iteration in range(ITERS):
        last = iteration + 1 == ITERS
        high, low = split(vector[...])
        vector_cat[:, 0:512] = high
        vector_cat[:, 512:1024] = high
        vector_cat[:, 1024:1536] = low
        for t in range(2):
            vector_stack[t, 0:128, :] = high[t * 128:(t + 1) * 128]
            vector_stack[t, 128:256, :] = low[t * 128:(t + 1) * 128]
        image[...] = jnp.dot(vector_cat[...], prior_cat[...], preferred_element_type=F32)

        @pl.loop(0, 8)
        def _(b):
            cover = covers[b] - first_tile

            @pl.when(jnp.logical_and(cover >= 0, cover < 2))
            def _():
                model[...] = jnp.dot(points[b], vector_stack[cover], preferred_element_type=F32)
                if last:
                    forms[...] += square_form(b, mixer, model)
                else:
                    apply_mixer(b, mixer, model, mixed)
                    high, low = split(mixed[...])
                    mixed_stack[0:128, :] = high
                    mixed_stack[128:256, :] = low
                    rows = pl.ds(pl.multiple_of(cover * 128, 128), 128)
                    image[rows, :] += jnp.dot(points_t[b], mixed_stack[...], preferred_element_type=F32)

        result = image[...]
        found = total(vector[...], result)
        if last:
            found = found + jnp.sum(forms[...], axis=0, keepdims=True)
        sums.append(found)
        if not last:
            following = scale[...] * result * factor
            vector[...] = following
            sums.append(total(following, result))
    sums = jnp.concatenate(sums, axis=0)
    for i in range(32):
        moment_ref[i] = sums


def steps_of(moments_ref, factor):
    sums = moments_ref[0]
    for i in range(1, 32):
        sums = sums + moments_ref[i]
    sums = jnp.broadcast_to(jnp.sum(sums, axis=1, keepdims=True), (8, 128))
    mu = [sums[n:n + 1, :] for n in range(8)]
    one = jnp.ones((1, 128), F32)
    norm = [one / jnp.sqrt(mu[2 * i + 1]) for i in range(4)]
    system = [[mu[i + j + 1] * norm[i] * norm[j] for j in range(4)] for i in range(4)]
    target = [(mu[0] if i == 0 else mu[i] * factor) * norm[i] for i in range(4)]
    lower = [[None] * 4 for _ in range(4)]
    inverse, pivot, forward = [None] * 4, [None] * 4, [None] * 4
    alphas, energies = [], []
    lead, sound = one, one > 0.0
    for i in range(4):
        for j in range(i):
            value = system[i][j]
            for m in range(j):
                value = value - lower[i][m] * lower[j][m] * pivot[m]
            lower[i][j] = value * inverse[j]
        value, aim = system[i][i], target[i]
        for m in range(i):
            value = value - lower[i][m] * lower[i][m] * pivot[m]
            aim = aim - lower[i][m] * forward[m]
        sound = jnp.logical_and(sound, value > 1e-6)
        pivot[i] = value
        inverse[i] = jnp.where(sound, one / value, 0.0)
        forward[i] = aim
        scaled = jnp.where(sound, lead / norm[i], one)
        alpha = aim * inverse[i] / scaled
        alphas.append(alpha)
        energies.append(alpha * scaled * scaled * pivot[i])
        sound = jnp.logical_and(sound, energies[i] > 0.0)
        lead = jnp.where(sound, -lead * alpha / factor, one)
        if i > 0:
            energies[i - 1] = jnp.where(sound, energies[i] / energies[i - 1], 0.0)
    return alphas, energies[:3]


def replay_kernel(covers, moments_ref, factor_ref, bands, squares, points, points_t, prior_cat, start_ref, scale,
                  right_ref, estimate_ref, residual_ref,
                  mixer, vector_cat, vector, carried, image, estimate, removed, model, mixed):
    first_tile = lax.axis_index("dish") * 2
    mine = choose_own()
    alphas, betas = steps_of(moments_ref, factor_ref[0:1, :])
    alphas = [value[0:1, 0:1] for value in alphas]
    betas = [value[0:1, 0:1] for value in betas]
    build_mixer(covers, bands, squares, mixer)
    vector[...] = start_ref[...]
    carried[...] = start_ref[...]
    for iteration in range(ITERS):
        high, low = split(vector[...])
        vector_cat[:, 0:512] = high
        vector_cat[:, 512:1024] = high
        vector_cat[:, 1024:1536] = low
        image[...] = jnp.dot(vector_cat[...], prior_cat[...], preferred_element_type=F32)

        @pl.loop(0, 8)
        def _(b):
            cover = covers[b] - first_tile

            @pl.when(jnp.logical_and(cover >= 0, cover < 2))
            def _():
                rows = pl.ds(pl.multiple_of(cover * 128, 128), 128)
                made = jnp.dot(points[b, :, 0:128], vector_cat[rows, 0:512], preferred_element_type=F32)
                model[...] = made.astype(BF16).astype(F32)
                apply_mixer(b, mixer, model, mixed)
                half = mixed[...].astype(BF16)
                image[rows, :] += jnp.dot(points_t[b, :, 0:128], half, preferred_element_type=F32)

        alpha = alphas[iteration]
        result = alpha * image[...]
        if iteration == 0:
            estimate[...] = alpha * vector[...]
            removed[...] = result
        else:
            estimate[...] = estimate[...] + alpha * vector[...]
            removed[...] = removed[...] + result
        if iteration + 1 < ITERS:
            moved = carried[...] - scale[...] * result
            carried[...] = moved
            vector[...] = moved + betas[iteration] * vector[...]
    high, low = split(estimate[...])
    estimate_ref[...] = dot_nt(mine, high) + dot_nt(mine, low)
    high, low = split(removed[...])
    residual_ref[...] = right_ref[...] - (dot_nt(mine, high) + dot_nt(mine, low))


def shape(dims, kind):
    return jax.ShapeDtypeStruct(dims, kind)


def body(time_data, pointing, coverage, noise_inv, gains, prior_inv, precond):
    spread = lax.all_gather(jnp.concatenate([precond, precond]), "freq", axis=0)
    packed = pl.pallas_call(
        prepare_kernel,
        out_shape=shape((592, 128), BF16),
        in_specs=[VMEM, VMEM, VMEM],
        out_specs=VMEM,
        scratch_shapes=[pltpu.VMEM((512, 128), F32)],
        name="prepare",
    )(time_data, noise_inv, jnp.swapaxes(gains, 1, 2))
    over_dish = lax.all_gather(packed, "dish", axis=0)
    own, square, ahead = pl.pallas_call(
        project_kernel,
        out_shape=(shape((64, 128), F32), shape((64, 128), BF16), shape((720, 128), BF16)),
        in_specs=[SMEM, VMEM, VMEM],
        out_specs=(VMEM, VMEM, VMEM),
        name="project",
    )(coverage, over_dish, pointing)
    count = lax.axis_size("tm")
    arrived = lax.ppermute(ahead, "tm", [(i, (i + 1) % count) for i in range(count)])
    prior_cat, bands, points, points_t, factor = pl.pallas_call(
        setup_kernel,
        out_shape=(shape((1536, 512), BF16), shape((DIAGS * 128, 128), BF16), shape((4, 128, 256), BF16),
                   shape((4, 128, 256), BF16), shape((8, 128), F32)),
        in_specs=[VMEM] * 3,
        out_specs=(VMEM,) * 5,
        cost_estimate=pl.CostEstimate(flops=200_000_000, bytes_accessed=6_000_000, transcendentals=0),
        name="setup",
    )(over_dish, prior_inv, pointing)
    right, packed = pl.pallas_call(
        start_kernel,
        out_shape=(shape((32, 256), F32), shape((SENT, 128), BF16)),
        in_specs=[VMEM] * 4,
        out_specs=(VMEM, VMEM),
        name="start",
    )(own, square, arrived, precond)
    over_freq = lax.all_gather(packed, "freq", axis=0)
    whole = (256, 512)
    moments, covers, scale, squares, points, points_t, first = pl.pallas_call(
        krylov_kernel,
        out_shape=(shape((32, 8, 128), F32), shape((8,), jnp.int32), shape(whole, F32), shape((8, 128, 512), BF16),
                   shape((8, 128, 256), BF16), shape((8, 128, 256), BF16), shape(whole, F32)),
        in_specs=[SMEM] + [VMEM] * 8,
        out_specs=(VMEM, SMEM) + (VMEM,) * 5,
        scratch_shapes=[
            pltpu.VMEM((8, DIAGS, 128, 512), F32),
            pltpu.VMEM((256, 1536), BF16),
            pltpu.VMEM((2, 256, 512), BF16),
            pltpu.VMEM(whole, F32),
            pltpu.VMEM(whole, F32),
            pltpu.VMEM((512, 256), F32),
            pltpu.VMEM((512, 128), BF16),
            pltpu.VMEM((512, 128), BF16),
            pltpu.VMEM((128, 512), F32),
            pltpu.VMEM((128, 512), F32),
            pltpu.VMEM(whole, BF16),
            pltpu.VMEM((8, 128), F32),
        ],
        compiler_params=pltpu.CompilerParams(vmem_limit_bytes=54 * 1024 * 1024),
        name="krylov",
    )(coverage, bands, over_freq, spread, prior_cat, points, points_t, factor, arrived)
    shared = lax.all_to_all(moments, ("tm", "dish"), split_axis=0, concat_axis=0)
    return tuple(pl.pallas_call(
        replay_kernel,
        out_shape=(shape((32, 256), F32), shape((32, 256), F32)),
        in_specs=[SMEM] + [VMEM] * 10,
        out_specs=(VMEM, VMEM),
        scratch_shapes=[
            pltpu.VMEM((8, DIAGS, 128, 512), F32),
            pltpu.VMEM((256, 1536), BF16),
            pltpu.VMEM(whole, F32),
            pltpu.VMEM(whole, F32),
            pltpu.VMEM(whole, F32),
            pltpu.VMEM(whole, F32),
            pltpu.VMEM(whole, F32),
            pltpu.VMEM((128, 512), F32),
            pltpu.VMEM((128, 512), F32),
        ],
        compiler_params=pltpu.CompilerParams(vmem_limit_bytes=54 * 1024 * 1024),
        name="replay",
    )(covers, shared, factor, bands, squares, points, points_t, prior_cat, first, scale, right))


def solution(mesh):
    return jax.shard_map(
        body,
        mesh=mesh,
        in_specs=(
            P("dish", "freq", "tm"),
            P("tm", None, None),
            P("tm"),
            P("dish", None, None),
            P("dish", "freq", "tm"),
            P(),
            P("freq", ("tm", "dish")),
        ),
        out_specs=(P("freq", ("tm", "dish")), P("freq", ("tm", "dish"))),
        check_vma=False,
    )
```

```python
import jax
import jax.numpy as jnp
from jax import lax
from jax.experimental import pallas as pl
from jax.experimental.pallas import tpu as pltpu
from jax.sharding import PartitionSpec as P

ITERS = 4
SENT = 254
CODES = 16383.0 / 0.9
DIAGS = 17
F32 = jnp.float32
BF16 = jnp.bfloat16
VMEM = pl.BlockSpec(memory_space=pltpu.VMEM)
SMEM = pl.BlockSpec(memory_space=pltpu.SMEM)


def split(x):
    high = x.astype(BF16)
    return high, (x - high.astype(F32)).astype(BF16)


def encode(gain):
    level = (gain - 1.0) * CODES
    count = jnp.floor(jnp.abs(level) + 0.5)
    place = jnp.floor(count * (1.0 / 128.0))
    value = 1.0 + (count - place * 128.0) * (1.0 / 128.0)
    value = value * 2.0 ** -63
    for step in (64, 32, 16, 8, 4, 2, 1):
        take = place >= step
        value = jnp.where(take, value * 2.0 ** step, value)
        place = jnp.where(take, place - step, place)
    return jnp.where(level < 0.0, -value, value)


def decode(code):
    value = jnp.abs(code)
    count = jnp.zeros_like(code)
    for step in (64, 32, 16, 8, 4, 2, 1):
        take = value >= 2.0 ** (step - 63)
        value = jnp.where(take, value * 2.0 ** -step, value)
        count = jnp.where(take, count + 128.0 * step, count)
    count = (count + (value * 2.0 ** 63 - 1.0) * 128.0) * (1.0 / CODES)
    return jnp.where(code < 0.0, 1.0 - count, 1.0 + count)


def dot_nt(a, b):
    return lax.dot_general(a, b, (((1,), (1,)), ((), ())), preferred_element_type=F32)


def prepare_kernel(data_ref, noise_ref, gain_ref, out_ref, band_ref):
    first_dish = lax.axis_index("dish") * 16
    lane = lax.broadcasted_iota(jnp.int32, (32, 128), 1)
    rows = lax.broadcasted_iota(jnp.int32, (32, 128), 0)
    pick = (lane == 127 - rows).astype(F32).astype(BF16)
    wide = lax.broadcasted_iota(jnp.int32, (128, 128), 1)
    tall = lax.broadcasted_iota(jnp.int32, (128, 128), 0)
    flip = (wide + tall == 127).astype(F32).astype(BF16)
    turned = [jnp.transpose(gain_ref[d]) for d in range(16)]
    rhs = [jnp.zeros((32, 128), F32) for _ in range(4)]
    squares = [jnp.zeros((32, 128), F32) for _ in range(2)]
    for d in range(16):
        noise = noise_ref[d]
        flipped = jnp.dot(noise, flip, preferred_element_type=F32)
        skewed = pltpu.roll(flipped, 0, 1, stride=1, stride_axis=0)
        band_ref[d * 32:(d + 1) * 32, :] = dot_nt(pick, skewed.astype(BF16))
        series = jnp.concatenate([data_ref[d, :, b * 128:(b + 1) * 128] for b in range(4)], axis=0)
        weighted = jnp.dot(series, noise, preferred_element_type=F32)
        for b in range(4):
            gain = jnp.broadcast_to(turned[d][:, b:b + 1], (32, 128))
            rhs[b] = rhs[b] + gain * weighted[b * 32:(b + 1) * 32]
            slot = (b % 2) * 64 + d + first_dish
            squares[b // 2] = jnp.where(lane == slot, gain, squares[b // 2])
    for k in range(DIAGS):
        out_ref[k * 16:(k + 1) * 16, :] = band_ref[pl.ds(k, 16, stride=32), :].astype(BF16)
    for b in range(4):
        high, low = split(rhs[b])
        out_ref[272 + b * 32:304 + b * 32, :] = high
        out_ref[400 + b * 32:432 + b * 32, :] = low
    for h in range(2):
        held = (lane & 63) - first_dish
        held = jnp.logical_and(held >= 0, held < 16)
        out_ref[528 + h * 32:560 + h * 32, :] = jnp.where(held, encode(squares[h]), 0.0).astype(BF16)


def project_kernel(cover_ref, gathered_ref, point_ref, own_ref, square_ref, ahead_ref):
    own = [jnp.zeros((32, 128), F32) for _ in range(2)]
    ahead = [jnp.zeros((32, 128), F32) for _ in range(2)]
    first_tile = lax.axis_index("dish") * 2
    lane = lax.broadcasted_iota(jnp.int32, (16, 128), 1)
    cover_row = jnp.zeros((16, 128), F32)
    for b in range(4):
        total = jnp.zeros((32, 128), F32)
        for j in range(4):
            total = total + gathered_ref[j, 272 + b * 32:304 + b * 32, :].astype(F32)
            total = total + gathered_ref[j, 400 + b * 32:432 + b * 32, :].astype(F32)
        part = jnp.dot(total.astype(BF16), point_ref[b], preferred_element_type=F32)
        tile = cover_ref[b]
        for t in range(2):
            own[t] = own[t] + jnp.where(tile == first_tile + t, part, 0.0)
            ahead[t] = ahead[t] + jnp.where(tile == first_tile + t + 8, part, 0.0)
        cover_row = jnp.where(lane == b, tile.astype(F32), cover_row)
        ahead_ref[192 + b * 128:320 + b * 128, :] = point_ref[b]
    square = jnp.zeros((64, 128), F32)
    for j in range(4):
        square = square + gathered_ref[j, 528:592, :].astype(F32)
    square_ref[...] = square.astype(BF16)
    ahead_ref[128:192, :] = square.astype(BF16)
    for t in range(2):
        own_ref[t * 32:(t + 1) * 32, :] = own[t]
        high, low = split(ahead[t])
        ahead_ref[t * 32:(t + 1) * 32, :] = high
        ahead_ref[64 + t * 32:96 + t * 32, :] = low
    ahead_ref[704:720, :] = cover_row.astype(BF16)


def start_kernel(own_ref, square_ref, arrived_ref, scale_ref, right_ref, out_ref):
    out_ref[64:128, :] = square_ref[...]
    out_ref[128:192, :] = arrived_ref[128:192, :]
    for t in range(2):
        rows = slice(t * 32, (t + 1) * 32)
        cols = slice(t * 128, (t + 1) * 128)
        right = (own_ref[rows, :] + arrived_ref[rows, :].astype(F32)
                 + arrived_ref[64 + t * 32:96 + t * 32, :].astype(F32))
        right_ref[:, cols] = right
        high, low = split(scale_ref[:, cols] * right)
        out_ref[rows, :] = high
        kept = SENT - 192 - t * 32 if t == 1 else 32
        out_ref[192 + t * 32:192 + t * 32 + kept, :] = low[:kept]


def unit(size):
    wide = lax.broadcasted_iota(jnp.int32, (size, size), 1)
    tall = lax.broadcasted_iota(jnp.int32, (size, size), 0)
    return (wide == tall).astype(F32).astype(BF16)


def woven():
    wide = lax.broadcasted_iota(jnp.int32, (128, 128), 1)
    tall = lax.broadcasted_iota(jnp.int32, (128, 128), 0)
    return (wide == (tall & 7) * 16 + (tall >> 3)).astype(F32).astype(BF16)


def weave_point(point, points, points_t, b):
    turn = woven()
    forward = jnp.dot(turn, point, preferred_element_type=F32).astype(BF16)
    flipped = dot_nt(unit(128), forward).astype(BF16)
    for half in range(2):
        points[b, :, half * 128:half * 128 + 128] = forward
        points_t[b, :, half * 128:half * 128 + 128] = flipped


def setup_kernel(noise_ref, prior_ref, point_ref, prior_cat, bands, points, points_t, factor_ref):
    turn = woven()
    prior = prior_ref[...]
    high, low = split(prior)
    prior_cat[0:512, :] = high
    prior_cat[512:1024, :] = low
    prior_cat[1024:1536, :] = high
    for k in range(DIAGS):
        piece = jnp.concatenate([noise_ref[j, k * 16:(k + 1) * 16, :] for j in range(4)] * 2, axis=0)
        bands[k * 128:(k + 1) * 128, :] = dot_nt(turn, piece).astype(BF16)
    for b in range(4):
        weave_point(point_ref[b], points, points_t, b)
    top = jnp.max(jnp.max(jnp.abs(prior), axis=0, keepdims=True), axis=1, keepdims=True)
    diag = jnp.zeros((16, 128), F32)
    for j in range(4):
        diag = diag + noise_ref[j, 0:16, :].astype(F32)
    level = jnp.sum(jnp.sum(diag, axis=0, keepdims=True), axis=1, keepdims=True) * (1.0 / 128.0)
    factor_ref[...] = jnp.broadcast_to(1.0 / (512.0 * (top + level)), (8, 128))


def choose_own():
    lane = lax.broadcasted_iota(jnp.int32, (32, 512), 1)
    line = lax.broadcasted_iota(jnp.int32, (32, 512), 0)
    return (lane == line + lax.axis_index("freq") * 32).astype(F32).astype(BF16)


def build_mixer(covers, bands, squares, mixer):
    first_tile = lax.axis_index("dish") * 2

    @pl.loop(0, 8)
    def _(b):
        cover = covers[b] - first_tile

        @pl.when(jnp.logical_and(cover >= 0, cover < 2))
        def _():
            square = squares[b]
            for k in range(DIAGS):
                made = jnp.dot(bands[k * 128:(k + 1) * 128, :], square, preferred_element_type=F32)
                for group in range(4):
                    for i in range(16):
                        row = (i * DIAGS + k) * 8
                        mixer[b, group, row:row + 8, :] = made[i * 8:(i + 1) * 8, group * 128:(group + 1) * 128]


def apply_mixer(b, mixer, model, mixed):
    @pl.loop(0, 4)
    def _(group):
        cols = pl.ds(pl.multiple_of(group * 128, 128), 128)
        near, sums = {}, {}

        def at(i):
            if i not in near:
                value = model[(i % 16) * 8:(i % 16) * 8 + 8, cols]
                near[i] = pltpu.roll(value, 7, 0) if i >= 16 else value
            return near[i]

        for i in range(16):
            own = at(i)
            weight = mixer[b, group, i * DIAGS * 8:i * DIAGS * 8 + 8, :]
            total = weight * own
            if i in sums:
                total = total + sums[i]
            for k in range(1, DIAGS):
                weight = mixer[b, group, (i * DIAGS + k) * 8:(i * DIAGS + k) * 8 + 8, :]
                total = total + weight * at(i + k)
                spill = weight * own
                sums[i + k] = sums[i + k] + spill if i + k in sums else spill
            mixed[i * 8:(i + 1) * 8, cols] = total
        for i in range(16):
            mixed[i * 8:(i + 1) * 8, cols] += pltpu.roll(sums[16 + i], 1, 0)


def square_form(b, mixer, model):
    def step(group, running):
        cols = pl.ds(pl.multiple_of(group * 128, 128), 128)
        near = {}

        def at(i):
            if i not in near:
                value = model[(i % 16) * 8:(i % 16) * 8 + 8, cols]
                near[i] = pltpu.roll(value, 7, 0) if i >= 16 else value
            return near[i]

        for i in range(16):
            own = at(i)
            value = mixer[b, group, i * DIAGS * 8 + 8:i * DIAGS * 8 + 16, :] * at(i + 1)
            for k in range(2, DIAGS):
                value = value + mixer[b, group, (i * DIAGS + k) * 8:(i * DIAGS + k) * 8 + 8, :] * at(i + k)
            value = 2.0 * value + mixer[b, group, i * DIAGS * 8:i * DIAGS * 8 + 8, :] * own
            running = running + value * own
        return running

    return lax.fori_loop(0, 4, step, jnp.zeros((8, 128), F32))


def assemble_kernel(cover_ref, gathered_ref, point_ref, flip_ref, arrived_ref,
                    covers, squares, points, points_t, start_ref, stage, stage_low):
    eye = unit(128)
    for q in range(4):
        for f in range(16):
            stage[f * 32:(f + 1) * 32, :] = gathered_ref[f, 64 + q * 32:96 + q * 32, :]
        gain = decode(stage[...].astype(F32))
        high, low = split(gain * gain)
        high, low = dot_nt(eye, high).astype(BF16), dot_nt(eye, low).astype(BF16)
        for side in range(2):
            squares[2 * q + side, 0:64, :] = high[side * 64:side * 64 + 64]
            squares[2 * q + side, 64:128, :] = low[side * 64:side * 64 + 64]
    for t in range(2):
        kept = SENT - 192 - t * 32 if t == 1 else 32
        stage_low[...] = jnp.zeros_like(stage_low)
        for f in range(16):
            stage[f * 32:(f + 1) * 32, :] = gathered_ref[f, t * 32:(t + 1) * 32, :]
            stage_low[f * 32:f * 32 + kept, :] = gathered_ref[f, 192 + t * 32:192 + t * 32 + kept, :]
        start_ref[t * 128:(t + 1) * 128, :] = dot_nt(eye, stage[...]) + dot_nt(eye, stage_low[...])
    row = arrived_ref[704:720, :].astype(F32)[0:1, :]
    spot = lax.broadcasted_iota(jnp.int32, (1, 128), 1)
    for b in range(4):
        covers[b] = cover_ref[b]
        covers[4 + b] = jnp.sum(jnp.where(spot == b, row, 0.0)).astype(jnp.int32) - 8
        points[b] = point_ref[b]
        points_t[b] = flip_ref[b]
        weave_point(arrived_ref[192 + b * 128:320 + b * 128, :], points, points_t, 4 + b)


def krylov_kernel(covers, bands, squares, points, points_t, start_ref, scales_ref, prior_cat, factor_ref,
                  moment_ref, scale,
                  mixer, vector_cat, vector_stack, vector, image, scale_rows, model, mixed, mixed_stack, forms):
    first_tile = lax.axis_index("dish") * 2
    vector[...] = start_ref[...]
    for f in range(16):
        scale_rows[f * 32:(f + 1) * 32, :] = scales_ref[f, 0:32, :]
    scale[...] = jnp.transpose(scale_rows[...])
    factor = factor_ref[0:1, 0:1]
    build_mixer(covers, bands, squares, mixer)

    def total(a, b):
        both = a * b
        both = both[:, 0:128] + both[:, 128:256] + (both[:, 256:384] + both[:, 384:512])
        return jnp.sum(both, axis=0, keepdims=True)

    forms[...] = jnp.zeros_like(forms)
    sums = [total(vector[...] * vector[...], 1.0 / scale[...])]
    for iteration in range(ITERS):
        last = iteration + 1 == ITERS
        high, low = split(vector[...])
        vector_cat[:, 0:512] = high
        vector_cat[:, 512:1024] = high
        vector_cat[:, 1024:1536] = low
        for t in range(2):
            vector_stack[t, 0:128, :] = high[t * 128:(t + 1) * 128]
            vector_stack[t, 128:256, :] = low[t * 128:(t + 1) * 128]
        image[...] = jnp.dot(vector_cat[...], prior_cat[...], preferred_element_type=F32)

        @pl.loop(0, 8)
        def _(b):
            cover = covers[b] - first_tile

            @pl.when(jnp.logical_and(cover >= 0, cover < 2))
            def _():
                model[...] = jnp.dot(points[b], vector_stack[cover], preferred_element_type=F32)
                if last:
                    forms[...] += square_form(b, mixer, model)
                else:
                    apply_mixer(b, mixer, model, mixed)
                    high, low = split(mixed[...])
                    mixed_stack[0:128, :] = high
                    mixed_stack[128:256, :] = low
                    rows = pl.ds(pl.multiple_of(cover * 128, 128), 128)
                    image[rows, :] += jnp.dot(points_t[b], mixed_stack[...], preferred_element_type=F32)

        result = image[...]
        found = total(vector[...], result)
        if last:
            found = found + jnp.sum(forms[...], axis=0, keepdims=True)
        sums.append(found)
        if not last:
            following = scale[...] * result * factor
            vector[...] = following
            sums.append(total(following, result))
    sums = jnp.concatenate(sums, axis=0)
    for i in range(32):
        moment_ref[i] = sums


def steps_of(moments_ref, factor):
    sums = moments_ref[0]
    for i in range(1, 32):
        sums = sums + moments_ref[i]
    sums = jnp.broadcast_to(jnp.sum(sums, axis=1, keepdims=True), (8, 128))
    mu = [sums[n:n + 1, :] for n in range(8)]
    one = jnp.ones((1, 128), F32)
    norm = [one / jnp.sqrt(mu[2 * i + 1]) for i in range(4)]
    system = [[mu[i + j + 1] * norm[i] * norm[j] for j in range(4)] for i in range(4)]
    target = [(mu[0] if i == 0 else mu[i] * factor) * norm[i] for i in range(4)]
    lower = [[None] * 4 for _ in range(4)]
    inverse, pivot, forward = [None] * 4, [None] * 4, [None] * 4
    alphas, energies = [], []
    lead, sound = one, one > 0.0
    for i in range(4):
        for j in range(i):
            value = system[i][j]
            for m in range(j):
                value = value - lower[i][m] * lower[j][m] * pivot[m]
            lower[i][j] = value * inverse[j]
        value, aim = system[i][i], target[i]
        for m in range(i):
            value = value - lower[i][m] * lower[i][m] * pivot[m]
            aim = aim - lower[i][m] * forward[m]
        sound = jnp.logical_and(sound, value > 1e-6)
        pivot[i] = value
        inverse[i] = jnp.where(sound, one / value, 0.0)
        forward[i] = aim
        scaled = jnp.where(sound, lead / norm[i], one)
        alpha = aim * inverse[i] / scaled
        alphas.append(alpha)
        energies.append(alpha * scaled * scaled * pivot[i])
        sound = jnp.logical_and(sound, energies[i] > 0.0)
        lead = jnp.where(sound, -lead * alpha / factor, one)
        if i > 0:
            energies[i - 1] = jnp.where(sound, energies[i] / energies[i - 1], 0.0)
    return alphas, energies[:3]


def replay_kernel(covers, moments_ref, factor_ref, bands, squares, points, points_t, prior_cat, start_ref, scale,
                  right_ref, estimate_ref, residual_ref,
                  mixer, vector_cat, vector, carried, image, estimate, removed, model, mixed):
    first_tile = lax.axis_index("dish") * 2
    mine = choose_own()
    alphas, betas = steps_of(moments_ref, factor_ref[0:1, :])
    alphas = [value[0:1, 0:1] for value in alphas]
    betas = [value[0:1, 0:1] for value in betas]
    build_mixer(covers, bands, squares, mixer)
    vector[...] = start_ref[...]
    carried[...] = start_ref[...]
    for iteration in range(ITERS):
        high, low = split(vector[...])
        vector_cat[:, 0:512] = high
        vector_cat[:, 512:1024] = high
        vector_cat[:, 1024:1536] = low
        image[...] = jnp.dot(vector_cat[...], prior_cat[...], preferred_element_type=F32)

        @pl.loop(0, 8)
        def _(b):
            cover = covers[b] - first_tile

            @pl.when(jnp.logical_and(cover >= 0, cover < 2))
            def _():
                rows = pl.ds(pl.multiple_of(cover * 128, 128), 128)
                made = jnp.dot(points[b, :, 0:128], vector_cat[rows, 0:512], preferred_element_type=F32)
                model[...] = made.astype(BF16).astype(F32)
                apply_mixer(b, mixer, model, mixed)
                half = mixed[...].astype(BF16)
                image[rows, :] += jnp.dot(points_t[b, :, 0:128], half, preferred_element_type=F32)

        alpha = alphas[iteration]
        result = alpha * image[...]
        if iteration == 0:
            estimate[...] = alpha * vector[...]
            removed[...] = result
        else:
            estimate[...] = estimate[...] + alpha * vector[...]
            removed[...] = removed[...] + result
        if iteration + 1 < ITERS:
            moved = carried[...] - scale[...] * result
            carried[...] = moved
            vector[...] = moved + betas[iteration] * vector[...]
    high, low = split(estimate[...])
    estimate_ref[...] = dot_nt(mine, high) + dot_nt(mine, low)
    high, low = split(removed[...])
    residual_ref[...] = right_ref[...] - (dot_nt(mine, high) + dot_nt(mine, low))


def shape(dims, kind):
    return jax.ShapeDtypeStruct(dims, kind)


def body(time_data, pointing, coverage, noise_inv, gains, prior_inv, precond):
    spread = lax.all_gather(jnp.concatenate([precond, precond]), "freq", axis=0)
    packed = pl.pallas_call(
        prepare_kernel,
        out_shape=shape((592, 128), BF16),
        in_specs=[VMEM, VMEM, VMEM],
        out_specs=VMEM,
        scratch_shapes=[pltpu.VMEM((512, 128), F32)],
        name="prepare",
    )(time_data, noise_inv, jnp.swapaxes(gains, 1, 2))
    over_dish = lax.all_gather(packed, "dish", axis=0)
    own, square, ahead = pl.pallas_call(
        project_kernel,
        out_shape=(shape((64, 128), F32), shape((64, 128), BF16), shape((720, 128), BF16)),
        in_specs=[SMEM, VMEM, VMEM],
        out_specs=(VMEM, VMEM, VMEM),
        name="project",
    )(coverage, over_dish, pointing)
    count = lax.axis_size("tm")
    arrived = lax.ppermute(ahead, "tm", [(i, (i + 1) % count) for i in range(count)])
    prior_cat, bands, points, points_t, factor = pl.pallas_call(
        setup_kernel,
        out_shape=(shape((1536, 512), BF16), shape((DIAGS * 128, 128), BF16), shape((4, 128, 256), BF16),
                   shape((4, 128, 256), BF16), shape((8, 128), F32)),
        in_specs=[VMEM] * 3,
        out_specs=(VMEM,) * 5,
        cost_estimate=pl.CostEstimate(flops=200_000_000, bytes_accessed=6_000_000, transcendentals=0),
        name="setup",
    )(over_dish, prior_inv, pointing)
    right, packed = pl.pallas_call(
        start_kernel,
        out_shape=(shape((32, 256), F32), shape((SENT, 128), BF16)),
        in_specs=[VMEM] * 4,
        out_specs=(VMEM, VMEM),
        name="start",
    )(own, square, arrived, precond)
    over_freq = lax.all_gather(packed, "freq", axis=0)
    whole = (256, 512)
    covers, squares, points, points_t, first = pl.pallas_call(
        assemble_kernel,
        out_shape=(shape((8,), jnp.int32), shape((8, 128, 512), BF16),
                   shape((8, 128, 256), BF16), shape((8, 128, 256), BF16), shape(whole, F32)),
        in_specs=[SMEM] + [VMEM] * 4,
        out_specs=(SMEM,) + (VMEM,) * 4,
        scratch_shapes=[pltpu.VMEM((512, 128), BF16), pltpu.VMEM((512, 128), BF16)],
        cost_estimate=pl.CostEstimate(flops=300_000_000, bytes_accessed=4_000_000, transcendentals=0),
        name="assemble",
    )(coverage, over_freq, points, points_t, arrived)
    moments, scale = pl.pallas_call(
        krylov_kernel,
        out_shape=(shape((32, 8, 128), F32), shape(whole, F32)),
        in_specs=[SMEM] + [VMEM] * 8,
        out_specs=(VMEM, VMEM),
        scratch_shapes=[
            pltpu.VMEM((8, 4, DIAGS * 128, 128), F32),
            pltpu.VMEM((256, 1536), BF16),
            pltpu.VMEM((2, 256, 512), BF16),
            pltpu.VMEM(whole, F32),
            pltpu.VMEM(whole, F32),
            pltpu.VMEM((512, 256), F32),
            pltpu.VMEM((128, 512), F32),
            pltpu.VMEM((128, 512), F32),
            pltpu.VMEM(whole, BF16),
            pltpu.VMEM((8, 128), F32),
        ],
        compiler_params=pltpu.CompilerParams(vmem_limit_bytes=54 * 1024 * 1024),
        name="krylov",
    )(covers, bands, squares, points, points_t, first, spread, prior_cat, factor)
    shared = lax.all_to_all(moments, ("tm", "dish"), split_axis=0, concat_axis=0)
    return tuple(pl.pallas_call(
        replay_kernel,
        out_shape=(shape((32, 256), F32), shape((32, 256), F32)),
        in_specs=[SMEM] + [VMEM] * 10,
        out_specs=(VMEM, VMEM),
        scratch_shapes=[
            pltpu.VMEM((8, 4, DIAGS * 128, 128), F32),
            pltpu.VMEM((256, 1536), BF16),
            pltpu.VMEM(whole, F32),
            pltpu.VMEM(whole, F32),
            pltpu.VMEM(whole, F32),
            pltpu.VMEM(whole, F32),
            pltpu.VMEM(whole, F32),
            pltpu.VMEM((128, 512), F32),
            pltpu.VMEM((128, 512), F32),
        ],
        compiler_params=pltpu.CompilerParams(vmem_limit_bytes=54 * 1024 * 1024),
        name="replay",
    )(covers, shared, factor, bands, squares, points, points_t, prior_cat, first, scale, right))


def solution(mesh):
    return jax.shard_map(
        body,
        mesh=mesh,
        in_specs=(
            P("dish", "freq", "tm"),
            P("tm", None, None),
            P("tm"),
            P("dish", None, None),
            P("dish", "freq", "tm"),
            P(),
            P("freq", ("tm", "dish")),
        ),
        out_specs=(P("freq", ("tm", "dish")), P("freq", ("tm", "dish"))),
        check_vma=False,
    )
```

```python
import jax
import jax.numpy as jnp
from jax import lax
from jax.experimental import pallas as pl
from jax.experimental.pallas import tpu as pltpu
from jax.sharding import PartitionSpec as P

ITERS = 4
SENT = 254
CODES = 16383.0 / 0.9
DIAGS = 17
F32 = jnp.float32
BF16 = jnp.bfloat16
VMEM = pl.BlockSpec(memory_space=pltpu.VMEM)
SMEM = pl.BlockSpec(memory_space=pltpu.SMEM)


def split(x):
    high = x.astype(BF16)
    return high, (x - high.astype(F32)).astype(BF16)


def encode(gain):
    level = (gain - 1.0) * CODES
    count = jnp.floor(jnp.abs(level) + 0.5)
    place = jnp.floor(count * (1.0 / 128.0))
    value = 1.0 + (count - place * 128.0) * (1.0 / 128.0)
    value = value * 2.0 ** -63
    for step in (64, 32, 16, 8, 4, 2, 1):
        take = place >= step
        value = jnp.where(take, value * 2.0 ** step, value)
        place = jnp.where(take, place - step, place)
    return jnp.where(level < 0.0, -value, value)


def decode(code):
    value = jnp.abs(code)
    count = jnp.zeros_like(code)
    for step in (64, 32, 16, 8, 4, 2, 1):
        take = value >= 2.0 ** (step - 63)
        value = jnp.where(take, value * 2.0 ** -step, value)
        count = jnp.where(take, count + 128.0 * step, count)
    count = (count + (value * 2.0 ** 63 - 1.0) * 128.0) * (1.0 / CODES)
    return jnp.where(code < 0.0, 1.0 - count, 1.0 + count)


def dot_nt(a, b):
    return lax.dot_general(a, b, (((1,), (1,)), ((), ())), preferred_element_type=F32)


def prepare_kernel(data_ref, noise_ref, gain_ref, out_ref, band_ref):
    first_dish = lax.axis_index("dish") * 16
    lane = lax.broadcasted_iota(jnp.int32, (32, 128), 1)
    rows = lax.broadcasted_iota(jnp.int32, (32, 128), 0)
    pick = (lane == 127 - rows).astype(F32).astype(BF16)
    wide = lax.broadcasted_iota(jnp.int32, (128, 128), 1)
    tall = lax.broadcasted_iota(jnp.int32, (128, 128), 0)
    flip = (wide + tall == 127).astype(F32).astype(BF16)
    turned = [jnp.transpose(gain_ref[d]) for d in range(16)]
    rhs = [jnp.zeros((32, 128), F32) for _ in range(4)]
    squares = [jnp.zeros((32, 128), F32) for _ in range(2)]
    for d in range(16):
        noise = noise_ref[d]
        flipped = jnp.dot(noise, flip, preferred_element_type=F32)
        skewed = pltpu.roll(flipped, 0, 1, stride=1, stride_axis=0)
        band_ref[d * 32:(d + 1) * 32, :] = dot_nt(pick, skewed.astype(BF16))
        series = jnp.concatenate([data_ref[d, :, b * 128:(b + 1) * 128] for b in range(4)], axis=0)
        weighted = jnp.dot(series, noise, preferred_element_type=F32)
        for b in range(4):
            gain = jnp.broadcast_to(turned[d][:, b:b + 1], (32, 128))
            rhs[b] = rhs[b] + gain * weighted[b * 32:(b + 1) * 32]
            slot = (b % 2) * 64 + d + first_dish
            squares[b // 2] = jnp.where(lane == slot, gain, squares[b // 2])
    for k in range(DIAGS):
        out_ref[k * 16:(k + 1) * 16, :] = band_ref[pl.ds(k, 16, stride=32), :].astype(BF16)
    for b in range(4):
        high, low = split(rhs[b])
        out_ref[272 + b * 32:304 + b * 32, :] = high
        out_ref[400 + b * 32:432 + b * 32, :] = low
    for h in range(2):
        held = (lane & 63) - first_dish
        held = jnp.logical_and(held >= 0, held < 16)
        out_ref[528 + h * 32:560 + h * 32, :] = jnp.where(held, encode(squares[h]), 0.0).astype(BF16)


def project_kernel(cover_ref, gathered_ref, point_ref, own_ref, square_ref, ahead_ref):
    own = [jnp.zeros((32, 128), F32) for _ in range(2)]
    ahead = [jnp.zeros((32, 128), F32) for _ in range(2)]
    first_tile = lax.axis_index("dish") * 2
    lane = lax.broadcasted_iota(jnp.int32, (16, 128), 1)
    cover_row = jnp.zeros((16, 128), F32)
    for b in range(4):
        total = jnp.zeros((32, 128), F32)
        for j in range(4):
            total = total + gathered_ref[j, 272 + b * 32:304 + b * 32, :].astype(F32)
            total = total + gathered_ref[j, 400 + b * 32:432 + b * 32, :].astype(F32)
        part = jnp.dot(total.astype(BF16), point_ref[b], preferred_element_type=F32)
        tile = cover_ref[b]
        for t in range(2):
            own[t] = own[t] + jnp.where(tile == first_tile + t, part, 0.0)
            ahead[t] = ahead[t] + jnp.where(tile == first_tile + t + 8, part, 0.0)
        cover_row = jnp.where(lane == b, tile.astype(F32), cover_row)
        ahead_ref[192 + b * 128:320 + b * 128, :] = point_ref[b]
    square = jnp.zeros((64, 128), F32)
    for j in range(4):
        square = square + gathered_ref[j, 528:592, :].astype(F32)
    square_ref[...] = square.astype(BF16)
    ahead_ref[128:192, :] = square.astype(BF16)
    for t in range(2):
        own_ref[t * 32:(t + 1) * 32, :] = own[t]
        high, low = split(ahead[t])
        ahead_ref[t * 32:(t + 1) * 32, :] = high
        ahead_ref[64 + t * 32:96 + t * 32, :] = low
    ahead_ref[704:720, :] = cover_row.astype(BF16)


def start_kernel(own_ref, square_ref, arrived_ref, scale_ref, right_ref, out_ref):
    out_ref[64:128, :] = square_ref[...]
    out_ref[128:192, :] = arrived_ref[128:192, :]
    for t in range(2):
        rows = slice(t * 32, (t + 1) * 32)
        cols = slice(t * 128, (t + 1) * 128)
        right = (own_ref[rows, :] + arrived_ref[rows, :].astype(F32)
                 + arrived_ref[64 + t * 32:96 + t * 32, :].astype(F32))
        right_ref[:, cols] = right
        high, low = split(scale_ref[:, cols] * right)
        out_ref[rows, :] = high
        kept = SENT - 192 - t * 32 if t == 1 else 32
        out_ref[192 + t * 32:192 + t * 32 + kept, :] = low[:kept]


def unit(size):
    wide = lax.broadcasted_iota(jnp.int32, (size, size), 1)
    tall = lax.broadcasted_iota(jnp.int32, (size, size), 0)
    return (wide == tall).astype(F32).astype(BF16)


def woven():
    wide = lax.broadcasted_iota(jnp.int32, (128, 128), 1)
    tall = lax.broadcasted_iota(jnp.int32, (128, 128), 0)
    return (wide == (tall & 7) * 16 + (tall >> 3)).astype(F32).astype(BF16)


def weave_point(point, points, points_t, b):
    turn = woven()
    forward = jnp.dot(turn, point, preferred_element_type=F32).astype(BF16)
    flipped = dot_nt(unit(128), forward).astype(BF16)
    for half in range(2):
        points[b, :, half * 128:half * 128 + 128] = forward
        points_t[b, :, half * 128:half * 128 + 128] = flipped


def setup_kernel(noise_ref, prior_ref, point_ref, prior_cat, bands, points, points_t, factor_ref):
    turn = woven()
    prior = prior_ref[...]
    high, low = split(prior)
    prior_cat[0:512, :] = high
    prior_cat[512:1024, :] = low
    prior_cat[1024:1536, :] = high
    for k in range(DIAGS):
        piece = jnp.concatenate([noise_ref[j, k * 16:(k + 1) * 16, :] for j in range(4)] * 2, axis=0)
        bands[k * 128:(k + 1) * 128, :] = dot_nt(turn, piece).astype(BF16)
    for b in range(4):
        weave_point(point_ref[b], points, points_t, b)
    top = jnp.max(jnp.max(jnp.abs(prior), axis=0, keepdims=True), axis=1, keepdims=True)
    diag = jnp.zeros((16, 128), F32)
    for j in range(4):
        diag = diag + noise_ref[j, 0:16, :].astype(F32)
    level = jnp.sum(jnp.sum(diag, axis=0, keepdims=True), axis=1, keepdims=True) * (1.0 / 128.0)
    factor_ref[...] = jnp.broadcast_to(1.0 / (512.0 * (top + level)), (8, 128))


def choose_own():
    lane = lax.broadcasted_iota(jnp.int32, (32, 512), 1)
    line = lax.broadcasted_iota(jnp.int32, (32, 512), 0)
    return (lane == line + lax.axis_index("freq") * 32).astype(F32).astype(BF16)


def build_mixer(covers, bands, squares, mixer):
    first_tile = lax.axis_index("dish") * 2

    @pl.loop(0, 8)
    def _(b):
        cover = covers[b] - first_tile

        @pl.when(jnp.logical_and(cover >= 0, cover < 2))
        def _():
            square = squares[b]
            for k in range(DIAGS):
                made = jnp.dot(bands[k * 128:(k + 1) * 128, :], square, preferred_element_type=F32)
                for group in range(4):
                    for i in range(16):
                        row = (i * DIAGS + k) * 8
                        mixer[b, group, row:row + 8, :] = made[i * 8:(i + 1) * 8, group * 128:(group + 1) * 128]


def apply_mixer(b, mixer, model, mixed):
    @pl.loop(0, 4)
    def _(group):
        cols = pl.ds(pl.multiple_of(group * 128, 128), 128)
        near, sums = {}, {}

        def at(i):
            if i not in near:
                value = model[(i % 16) * 8:(i % 16) * 8 + 8, cols]
                near[i] = pltpu.roll(value, 7, 0) if i >= 16 else value
            return near[i]

        for i in range(16):
            own = at(i)
            weight = mixer[b, group, i * DIAGS * 8:i * DIAGS * 8 + 8, :]
            total = weight * own
            if i in sums:
                total = total + sums[i]
            for k in range(1, DIAGS):
                weight = mixer[b, group, (i * DIAGS + k) * 8:(i * DIAGS + k) * 8 + 8, :]
                total = total + weight * at(i + k)
                spill = weight * own
                sums[i + k] = sums[i + k] + spill if i + k in sums else spill
            mixed[i * 8:(i + 1) * 8, cols] = total
        for i in range(16):
            mixed[i * 8:(i + 1) * 8, cols] += pltpu.roll(sums[16 + i], 1, 0)


def square_form(b, mixer, model):
    def step(group, running):
        cols = pl.ds(pl.multiple_of(group * 128, 128), 128)
        near = {}

        def at(i):
            if i not in near:
                value = model[(i % 16) * 8:(i % 16) * 8 + 8, cols]
                near[i] = pltpu.roll(value, 7, 0) if i >= 16 else value
            return near[i]

        for i in range(16):
            own = at(i)
            value = mixer[b, group, i * DIAGS * 8 + 8:i * DIAGS * 8 + 16, :] * at(i + 1)
            for k in range(2, DIAGS):
                value = value + mixer[b, group, (i * DIAGS + k) * 8:(i * DIAGS + k) * 8 + 8, :] * at(i + k)
            value = 2.0 * value + mixer[b, group, i * DIAGS * 8:i * DIAGS * 8 + 8, :] * own
            running = running + value * own
        return running

    return lax.fori_loop(0, 4, step, jnp.zeros((8, 128), F32))


def assemble_kernel(cover_ref, gathered_ref, point_ref, flip_ref, arrived_ref,
                    covers, squares, points, points_t, start_ref, stage, stage_low):
    eye = unit(128)
    for q in range(4):
        for f in range(16):
            stage[f * 32:(f + 1) * 32, :] = gathered_ref[f, 64 + q * 32:96 + q * 32, :]
        gain = decode(stage[...].astype(F32))
        high, low = split(gain * gain)
        high, low = dot_nt(eye, high).astype(BF16), dot_nt(eye, low).astype(BF16)
        for side in range(2):
            squares[2 * q + side, 0:64, :] = high[side * 64:side * 64 + 64]
            squares[2 * q + side, 64:128, :] = low[side * 64:side * 64 + 64]
    for t in range(2):
        kept = SENT - 192 - t * 32 if t == 1 else 32
        stage_low[...] = jnp.zeros_like(stage_low)
        for f in range(16):
            stage[f * 32:(f + 1) * 32, :] = gathered_ref[f, t * 32:(t + 1) * 32, :]
            stage_low[f * 32:f * 32 + kept, :] = gathered_ref[f, 192 + t * 32:192 + t * 32 + kept, :]
        start_ref[t * 128:(t + 1) * 128, :] = dot_nt(eye, stage[...]) + dot_nt(eye, stage_low[...])
    row = arrived_ref[704:720, :].astype(F32)[0:1, :]
    spot = lax.broadcasted_iota(jnp.int32, (1, 128), 1)
    for b in range(4):
        covers[b] = cover_ref[b]
        covers[4 + b] = jnp.sum(jnp.where(spot == b, row, 0.0)).astype(jnp.int32) - 8
        points[b] = point_ref[b]
        points_t[b] = flip_ref[b]
        weave_point(arrived_ref[192 + b * 128:320 + b * 128, :], points, points_t, 4 + b)


def krylov_kernel(covers, bands, squares, points, points_t, start_ref, scales_ref, prior_cat, factor_ref,
                  moment_ref, scale,
                  mixer, vector_cat, vector_stack, vector, image, scale_rows, model, mixed, mixed_stack, forms):
    first_tile = lax.axis_index("dish") * 2
    vector[...] = start_ref[...]
    for f in range(16):
        scale_rows[f * 32:(f + 1) * 32, :] = scales_ref[f, 0:32, :]
    scale[...] = jnp.transpose(scale_rows[...])
    factor = factor_ref[0:1, 0:1]
    build_mixer(covers, bands, squares, mixer)

    def total(a, b):
        both = a * b
        both = both[:, 0:128] + both[:, 128:256] + (both[:, 256:384] + both[:, 384:512])
        return jnp.sum(both, axis=0, keepdims=True)

    forms[...] = jnp.zeros_like(forms)
    sums = [total(vector[...] * vector[...], 1.0 / scale[...])]
    for iteration in range(ITERS):
        last = iteration + 1 == ITERS
        high, low = split(vector[...])
        vector_cat[:, 0:512] = high
        vector_cat[:, 512:1024] = high
        vector_cat[:, 1024:1536] = low
        for t in range(2):
            vector_stack[t, 0:128, :] = high[t * 128:(t + 1) * 128]
            vector_stack[t, 128:256, :] = low[t * 128:(t + 1) * 128]
        image[...] = jnp.dot(vector_cat[...], prior_cat[...], preferred_element_type=F32)

        @pl.loop(0, 8)
        def _(b):
            cover = covers[b] - first_tile

            @pl.when(jnp.logical_and(cover >= 0, cover < 2))
            def _():
                model[...] = jnp.dot(points[b], vector_stack[cover], preferred_element_type=F32)
                if last:
                    forms[...] += square_form(b, mixer, model)
                else:
                    apply_mixer(b, mixer, model, mixed)
                    high, low = split(mixed[...])
                    mixed_stack[0:128, :] = high
                    mixed_stack[128:256, :] = low
                    rows = pl.ds(pl.multiple_of(cover * 128, 128), 128)
                    image[rows, :] += jnp.dot(points_t[b], mixed_stack[...], preferred_element_type=F32)

        result = image[...]
        found = total(vector[...], result)
        if last:
            found = found + jnp.sum(forms[...], axis=0, keepdims=True)
        sums.append(found)
        if not last:
            following = scale[...] * result * factor
            vector[...] = following
            sums.append(total(following, result))
    sums = jnp.concatenate(sums, axis=0)
    for i in range(32):
        moment_ref[i] = sums


def steps_of(moments_ref, factor):
    sums = moments_ref[0]
    for i in range(1, 32):
        sums = sums + moments_ref[i]
    sums = jnp.broadcast_to(jnp.sum(sums, axis=1, keepdims=True), (8, 128))
    mu = [sums[n:n + 1, :] for n in range(8)]
    one = jnp.ones((1, 128), F32)
    norm = [one / jnp.sqrt(mu[2 * i + 1]) for i in range(4)]
    system = [[mu[i + j + 1] * norm[i] * norm[j] for j in range(4)] for i in range(4)]
    target = [(mu[0] if i == 0 else mu[i] * factor) * norm[i] for i in range(4)]
    lower = [[None] * 4 for _ in range(4)]
    inverse, pivot, forward = [None] * 4, [None] * 4, [None] * 4
    alphas, energies = [], []
    lead, sound = one, one > 0.0
    for i in range(4):
        for j in range(i):
            value = system[i][j]
            for m in range(j):
                value = value - lower[i][m] * lower[j][m] * pivot[m]
            lower[i][j] = value * inverse[j]
        value, aim = system[i][i], target[i]
        for m in range(i):
            value = value - lower[i][m] * lower[i][m] * pivot[m]
            aim = aim - lower[i][m] * forward[m]
        sound = jnp.logical_and(sound, value > 1e-6)
        pivot[i] = value
        inverse[i] = jnp.where(sound, one / value, 0.0)
        forward[i] = aim
        scaled = jnp.where(sound, lead / norm[i], one)
        alpha = aim * inverse[i] / scaled
        alphas.append(alpha)
        energies.append(alpha * scaled * scaled * pivot[i])
        sound = jnp.logical_and(sound, energies[i] > 0.0)
        lead = jnp.where(sound, -lead * alpha / factor, one)
        if i > 0:
            energies[i - 1] = jnp.where(sound, energies[i] / energies[i - 1], 0.0)
    return alphas, energies[:3]


def replay_kernel(covers, moments_ref, factor_ref, bands, squares, points, points_t, prior_cat, start_ref, scale,
                  right_ref, estimate_ref, residual_ref,
                  mixer, vector_cat, vector, carried, image, estimate, removed, model, mixed):
    first_tile = lax.axis_index("dish") * 2
    mine = choose_own()
    alphas, betas = steps_of(moments_ref, factor_ref[0:1, :])
    alphas = [value[0:1, 0:1] for value in alphas]
    betas = [value[0:1, 0:1] for value in betas]
    build_mixer(covers, bands, squares, mixer)
    vector[...] = start_ref[...]
    carried[...] = start_ref[...]
    for iteration in range(ITERS):
        high, low = split(vector[...])
        vector_cat[:, 0:512] = high
        vector_cat[:, 512:1024] = high
        vector_cat[:, 1024:1536] = low
        image[...] = jnp.dot(vector_cat[...], prior_cat[...], preferred_element_type=F32)

        @pl.loop(0, 8)
        def _(b):
            cover = covers[b] - first_tile

            @pl.when(jnp.logical_and(cover >= 0, cover < 2))
            def _():
                rows = pl.ds(pl.multiple_of(cover * 128, 128), 128)
                made = jnp.dot(points[b, :, 0:128], vector_cat[rows, 0:512], preferred_element_type=F32)
                model[...] = made.astype(BF16).astype(F32)
                apply_mixer(b, mixer, model, mixed)
                half = mixed[...].astype(BF16)
                image[rows, :] += jnp.dot(points_t[b, :, 0:128], half, preferred_element_type=F32)

        alpha = alphas[iteration]
        result = alpha * image[...]
        if iteration == 0:
            estimate[...] = alpha * vector[...]
            removed[...] = result
        else:
            estimate[...] = estimate[...] + alpha * vector[...]
            removed[...] = removed[...] + result
        if iteration + 1 < ITERS:
            moved = carried[...] - scale[...] * result
            carried[...] = moved
            vector[...] = moved + betas[iteration] * vector[...]
    high, low = split(estimate[...])
    estimate_ref[...] = dot_nt(mine, high) + dot_nt(mine, low)
    high, low = split(removed[...])
    residual_ref[...] = right_ref[...] - (dot_nt(mine, high) + dot_nt(mine, low))


def shape(dims, kind):
    return jax.ShapeDtypeStruct(dims, kind)


def body(time_data, pointing, coverage, noise_inv, gains, prior_inv, precond):
    spread = lax.all_gather(jnp.concatenate([precond, precond]), "freq", axis=0)
    packed = pl.pallas_call(
        prepare_kernel,
        out_shape=shape((592, 128), BF16),
        in_specs=[VMEM, VMEM, VMEM],
        out_specs=VMEM,
        scratch_shapes=[pltpu.VMEM((512, 128), F32)],
        compiler_params=pltpu.CompilerParams(vmem_limit_bytes=10 * 1024 * 1024),
        name="prepare",
    )(time_data, noise_inv, jnp.swapaxes(gains, 1, 2))
    over_dish = lax.all_gather(packed, "dish", axis=0)
    own, square, ahead = pl.pallas_call(
        project_kernel,
        out_shape=(shape((64, 128), F32), shape((64, 128), BF16), shape((720, 128), BF16)),
        in_specs=[SMEM, VMEM, VMEM],
        out_specs=(VMEM, VMEM, VMEM),
        compiler_params=pltpu.CompilerParams(vmem_limit_bytes=6 * 1024 * 1024),
        name="project",
    )(coverage, over_dish, pointing)
    count = lax.axis_size("tm")
    arrived = lax.ppermute(ahead, "tm", [(i, (i + 1) % count) for i in range(count)])
    prior_cat, bands, points, points_t, factor = pl.pallas_call(
        setup_kernel,
        out_shape=(shape((1536, 512), BF16), shape((DIAGS * 128, 128), BF16), shape((4, 128, 256), BF16),
                   shape((4, 128, 256), BF16), shape((8, 128), F32)),
        in_specs=[VMEM] * 3,
        out_specs=(VMEM,) * 5,
        cost_estimate=pl.CostEstimate(flops=200_000_000, bytes_accessed=6_000_000, transcendentals=0),
        compiler_params=pltpu.CompilerParams(vmem_limit_bytes=14 * 1024 * 1024),
        name="setup",
    )(over_dish, prior_inv, pointing)
    right, packed = pl.pallas_call(
        start_kernel,
        out_shape=(shape((32, 256), F32), shape((SENT, 128), BF16)),
        in_specs=[VMEM] * 4,
        out_specs=(VMEM, VMEM),
        compiler_params=pltpu.CompilerParams(vmem_limit_bytes=4 * 1024 * 1024),
        name="start",
    )(own, square, arrived, precond)
    over_freq = lax.all_gather(packed, "freq", axis=0)
    whole = (256, 512)
    covers, squares, points, points_t, first = pl.pallas_call(
        assemble_kernel,
        out_shape=(shape((8,), jnp.int32), shape((8, 128, 512), BF16),
                   shape((8, 128, 256), BF16), shape((8, 128, 256), BF16), shape(whole, F32)),
        in_specs=[SMEM] + [VMEM] * 4,
        out_specs=(SMEM,) + (VMEM,) * 4,
        scratch_shapes=[pltpu.VMEM((512, 128), BF16), pltpu.VMEM((512, 128), BF16)],
        cost_estimate=pl.CostEstimate(flops=300_000_000, bytes_accessed=4_000_000, transcendentals=0),
        compiler_params=pltpu.CompilerParams(vmem_limit_bytes=12 * 1024 * 1024),
        name="assemble",
    )(coverage, over_freq, points, points_t, arrived)
    moments, scale = pl.pallas_call(
        krylov_kernel,
        out_shape=(shape((32, 8, 128), F32), shape(whole, F32)),
        in_specs=[SMEM] + [VMEM] * 8,
        out_specs=(VMEM, VMEM),
        scratch_shapes=[
            pltpu.VMEM((8, 4, DIAGS * 128, 128), F32),
            pltpu.VMEM((256, 1536), BF16),
            pltpu.VMEM((2, 256, 512), BF16),
            pltpu.VMEM(whole, F32),
            pltpu.VMEM(whole, F32),
            pltpu.VMEM((512, 256), F32),
            pltpu.VMEM((128, 512), F32),
            pltpu.VMEM((128, 512), F32),
            pltpu.VMEM(whole, BF16),
            pltpu.VMEM((8, 128), F32),
        ],
        compiler_params=pltpu.CompilerParams(vmem_limit_bytes=50 * 1024 * 1024),
        name="krylov",
    )(covers, bands, squares, points, points_t, first, spread, prior_cat, factor)
    shared = lax.all_to_all(moments, ("tm", "dish"), split_axis=0, concat_axis=0)
    return tuple(pl.pallas_call(
        replay_kernel,
        out_shape=(shape((32, 256), F32), shape((32, 256), F32)),
        in_specs=[SMEM] + [VMEM] * 10,
        out_specs=(VMEM, VMEM),
        scratch_shapes=[
            pltpu.VMEM((8, 4, DIAGS * 128, 128), F32),
            pltpu.VMEM((256, 1536), BF16),
            pltpu.VMEM(whole, F32),
            pltpu.VMEM(whole, F32),
            pltpu.VMEM(whole, F32),
            pltpu.VMEM(whole, F32),
            pltpu.VMEM(whole, F32),
            pltpu.VMEM((128, 512), F32),
            pltpu.VMEM((128, 512), F32),
        ],
        compiler_params=pltpu.CompilerParams(vmem_limit_bytes=50 * 1024 * 1024),
        name="replay",
    )(covers, shared, factor, bands, squares, points, points_t, prior_cat, first, scale, right))


def solution(mesh):
    return jax.shard_map(
        body,
        mesh=mesh,
        in_specs=(
            P("dish", "freq", "tm"),
            P("tm", None, None),
            P("tm"),
            P("dish", None, None),
            P("dish", "freq", "tm"),
            P(),
            P("freq", ("tm", "dish")),
        ),
        out_specs=(P("freq", ("tm", "dish")), P("freq", ("tm", "dish"))),
        check_vma=False,
    )
```

```python
import jax
import jax.numpy as jnp
from jax import lax
from jax.experimental import pallas as pl
from jax.experimental.pallas import tpu as pltpu
from jax.sharding import PartitionSpec as P

ITERS = 4
SENT = 254
CODES = 16383.0 / 0.9
DIAGS = 17
F32 = jnp.float32
BF16 = jnp.bfloat16
VMEM = pl.BlockSpec(memory_space=pltpu.VMEM)
SMEM = pl.BlockSpec(memory_space=pltpu.SMEM)


def split(x):
    high = x.astype(BF16)
    return high, (x - high.astype(F32)).astype(BF16)


def encode(gain):
    level = (gain - 1.0) * CODES
    count = jnp.floor(jnp.abs(level) + 0.5)
    place = jnp.floor(count * (1.0 / 128.0))
    value = 1.0 + (count - place * 128.0) * (1.0 / 128.0)
    value = value * 2.0 ** -63
    for step in (64, 32, 16, 8, 4, 2, 1):
        take = place >= step
        value = jnp.where(take, value * 2.0 ** step, value)
        place = jnp.where(take, place - step, place)
    return jnp.where(level < 0.0, -value, value)


def decode(code):
    value = jnp.abs(code)
    count = jnp.zeros_like(code)
    for step in (64, 32, 16, 8, 4, 2, 1):
        take = value >= 2.0 ** (step - 63)
        value = jnp.where(take, value * 2.0 ** -step, value)
        count = jnp.where(take, count + 128.0 * step, count)
    count = (count + (value * 2.0 ** 63 - 1.0) * 128.0) * (1.0 / CODES)
    return jnp.where(code < 0.0, 1.0 - count, 1.0 + count)


def dot_nt(a, b):
    return lax.dot_general(a, b, (((1,), (1,)), ((), ())), preferred_element_type=F32)


def prepare_kernel(data_ref, noise_ref, gain_ref, out_ref, band_ref):
    first_dish = lax.axis_index("dish") * 16
    lane = lax.broadcasted_iota(jnp.int32, (32, 128), 1)
    rows = lax.broadcasted_iota(jnp.int32, (32, 128), 0)
    pick = (lane == 127 - rows).astype(F32).astype(BF16)
    wide = lax.broadcasted_iota(jnp.int32, (128, 128), 1)
    tall = lax.broadcasted_iota(jnp.int32, (128, 128), 0)
    flip = (wide + tall == 127).astype(F32).astype(BF16)
    turned = [jnp.transpose(gain_ref[d]) for d in range(16)]
    rhs = [jnp.zeros((32, 128), F32) for _ in range(4)]
    squares = [jnp.zeros((32, 128), F32) for _ in range(2)]
    for d in range(16):
        noise = noise_ref[d]
        flipped = jnp.dot(noise, flip, preferred_element_type=F32)
        skewed = pltpu.roll(flipped, 0, 1, stride=1, stride_axis=0)
        band_ref[d * 32:(d + 1) * 32, :] = dot_nt(pick, skewed.astype(BF16))
        series = jnp.concatenate([data_ref[d, :, b * 128:(b + 1) * 128] for b in range(4)], axis=0)
        weighted = jnp.dot(series, noise, preferred_element_type=F32)
        for b in range(4):
            gain = jnp.broadcast_to(turned[d][:, b:b + 1], (32, 128))
            rhs[b] = rhs[b] + gain * weighted[b * 32:(b + 1) * 32]
            slot = (b % 2) * 64 + d + first_dish
            squares[b // 2] = jnp.where(lane == slot, gain, squares[b // 2])
    for k in range(DIAGS):
        out_ref[k * 16:(k + 1) * 16, :] = band_ref[pl.ds(k, 16, stride=32), :].astype(BF16)
    for b in range(4):
        high, low = split(rhs[b])
        out_ref[272 + b * 32:304 + b * 32, :] = high
        out_ref[400 + b * 32:432 + b * 32, :] = low
    for h in range(2):
        held = (lane & 63) - first_dish
        held = jnp.logical_and(held >= 0, held < 16)
        out_ref[528 + h * 32:560 + h * 32, :] = jnp.where(held, encode(squares[h]), 0.0).astype(BF16)


def project_kernel(cover_ref, gathered_ref, point_ref, own_ref, square_ref, ahead_ref):
    own = [jnp.zeros((32, 128), F32) for _ in range(2)]
    ahead = [jnp.zeros((32, 128), F32) for _ in range(2)]
    first_tile = lax.axis_index("dish") * 2
    lane = lax.broadcasted_iota(jnp.int32, (16, 128), 1)
    cover_row = jnp.zeros((16, 128), F32)
    for b in range(4):
        total = jnp.zeros((32, 128), F32)
        for j in range(4):
            total = total + gathered_ref[j, 272 + b * 32:304 + b * 32, :].astype(F32)
            total = total + gathered_ref[j, 400 + b * 32:432 + b * 32, :].astype(F32)
        part = jnp.dot(total.astype(BF16), point_ref[b], preferred_element_type=F32)
        tile = cover_ref[b]
        for t in range(2):
            own[t] = own[t] + jnp.where(tile == first_tile + t, part, 0.0)
            ahead[t] = ahead[t] + jnp.where(tile == first_tile + t + 8, part, 0.0)
        cover_row = jnp.where(lane == b, tile.astype(F32), cover_row)
        ahead_ref[192 + b * 128:320 + b * 128, :] = point_ref[b]
    square = jnp.zeros((64, 128), F32)
    for j in range(4):
        square = square + gathered_ref[j, 528:592, :].astype(F32)
    square_ref[...] = square.astype(BF16)
    ahead_ref[128:192, :] = square.astype(BF16)
    for t in range(2):
        own_ref[t * 32:(t + 1) * 32, :] = own[t]
        high, low = split(ahead[t])
        ahead_ref[t * 32:(t + 1) * 32, :] = high
        ahead_ref[64 + t * 32:96 + t * 32, :] = low
    ahead_ref[704:720, :] = cover_row.astype(BF16)


def start_kernel(own_ref, square_ref, arrived_ref, scale_ref, right_ref, out_ref):
    out_ref[64:128, :] = square_ref[...]
    out_ref[128:192, :] = arrived_ref[128:192, :]
    for t in range(2):
        rows = slice(t * 32, (t + 1) * 32)
        cols = slice(t * 128, (t + 1) * 128)
        right = (own_ref[rows, :] + arrived_ref[rows, :].astype(F32)
                 + arrived_ref[64 + t * 32:96 + t * 32, :].astype(F32))
        right_ref[:, cols] = right
        high, low = split(scale_ref[:, cols] * right)
        out_ref[rows, :] = high
        kept = SENT - 192 - t * 32 if t == 1 else 32
        out_ref[192 + t * 32:192 + t * 32 + kept, :] = low[:kept]


def unit(size):
    wide = lax.broadcasted_iota(jnp.int32, (size, size), 1)
    tall = lax.broadcasted_iota(jnp.int32, (size, size), 0)
    return (wide == tall).astype(F32).astype(BF16)


def woven():
    wide = lax.broadcasted_iota(jnp.int32, (128, 128), 1)
    tall = lax.broadcasted_iota(jnp.int32, (128, 128), 0)
    return (wide == (tall & 7) * 16 + (tall >> 3)).astype(F32).astype(BF16)


def weave_point(point, points, points_t, b):
    turn = woven()
    forward = jnp.dot(turn, point, preferred_element_type=F32).astype(BF16)
    flipped = dot_nt(unit(128), forward).astype(BF16)
    for half in range(2):
        points[b, :, half * 128:half * 128 + 128] = forward
        points_t[b, :, half * 128:half * 128 + 128] = flipped


def setup_kernel(noise_ref, prior_ref, point_ref, prior_cat, bands, points, points_t, factor_ref):
    turn = woven()
    prior = prior_ref[...]
    high, low = split(prior)
    prior_cat[0:512, :] = high
    prior_cat[512:1024, :] = low
    prior_cat[1024:1536, :] = high
    for k in range(DIAGS):
        piece = jnp.concatenate([noise_ref[j, k * 16:(k + 1) * 16, :] for j in range(4)] * 2, axis=0)
        bands[k * 128:(k + 1) * 128, :] = dot_nt(turn, piece).astype(BF16)
    for b in range(4):
        weave_point(point_ref[b], points, points_t, b)
    top = jnp.max(jnp.max(jnp.abs(prior), axis=0, keepdims=True), axis=1, keepdims=True)
    diag = jnp.zeros((16, 128), F32)
    for j in range(4):
        diag = diag + noise_ref[j, 0:16, :].astype(F32)
    level = jnp.sum(jnp.sum(diag, axis=0, keepdims=True), axis=1, keepdims=True) * (1.0 / 128.0)
    factor_ref[...] = jnp.broadcast_to(1.0 / (512.0 * (top + level)), (8, 128))


def choose_own():
    lane = lax.broadcasted_iota(jnp.int32, (32, 512), 1)
    line = lax.broadcasted_iota(jnp.int32, (32, 512), 0)
    return (lane == line + lax.axis_index("freq") * 32).astype(F32).astype(BF16)


def build_mixer(covers, bands, squares, mixer):
    first_tile = lax.axis_index("dish") * 2

    @pl.loop(0, 8)
    def _(b):
        cover = covers[b] - first_tile

        @pl.when(jnp.logical_and(cover >= 0, cover < 2))
        def _():
            square = squares[b]
            for k in range(DIAGS):
                made = jnp.dot(bands[k * 128:(k + 1) * 128, :], square, preferred_element_type=F32)
                for group in range(4):
                    for i in range(16):
                        row = (i * DIAGS + k) * 8
                        mixer[b, group, row:row + 8, :] = made[i * 8:(i + 1) * 8, group * 128:(group + 1) * 128]


def apply_mixer(b, mixer, model, mixed):
    @pl.loop(0, 4)
    def _(group):
        cols = pl.ds(pl.multiple_of(group * 128, 128), 128)
        near, sums = {}, {}

        def at(i):
            if i not in near:
                value = model[(i % 16) * 8:(i % 16) * 8 + 8, cols]
                near[i] = pltpu.roll(value, 7, 0) if i >= 16 else value
            return near[i]

        for i in range(16):
            own = at(i)
            weight = mixer[b, group, i * DIAGS * 8:i * DIAGS * 8 + 8, :]
            total = weight * own
            if i in sums:
                total = total + sums[i]
            for k in range(1, DIAGS):
                weight = mixer[b, group, (i * DIAGS + k) * 8:(i * DIAGS + k) * 8 + 8, :]
                total = total + weight * at(i + k)
                spill = weight * own
                sums[i + k] = sums[i + k] + spill if i + k in sums else spill
            mixed[i * 8:(i + 1) * 8, cols] = total
        for i in range(16):
            mixed[i * 8:(i + 1) * 8, cols] += pltpu.roll(sums[16 + i], 1, 0)


def square_form(b, mixer, model):
    def step(group, running):
        cols = pl.ds(pl.multiple_of(group * 128, 128), 128)
        near = {}

        def at(i):
            if i not in near:
                value = model[(i % 16) * 8:(i % 16) * 8 + 8, cols]
                near[i] = pltpu.roll(value, 7, 0) if i >= 16 else value
            return near[i]

        for i in range(16):
            own = at(i)
            value = mixer[b, group, i * DIAGS * 8 + 8:i * DIAGS * 8 + 16, :] * at(i + 1)
            for k in range(2, DIAGS):
                value = value + mixer[b, group, (i * DIAGS + k) * 8:(i * DIAGS + k) * 8 + 8, :] * at(i + k)
            value = 2.0 * value + mixer[b, group, i * DIAGS * 8:i * DIAGS * 8 + 8, :] * own
            running = running + value * own
        return running

    return lax.fori_loop(0, 4, step, jnp.zeros((8, 128), F32))


def assemble_kernel(cover_ref, gathered_ref, point_ref, flip_ref, arrived_ref,
                    covers, squares, points, points_t, start_ref, stage, stage_low):
    eye = unit(128)
    for q in range(4):
        for f in range(16):
            stage[f * 32:(f + 1) * 32, :] = gathered_ref[f, 64 + q * 32:96 + q * 32, :]
        gain = decode(stage[...].astype(F32))
        high, low = split(gain * gain)
        high, low = dot_nt(eye, high).astype(BF16), dot_nt(eye, low).astype(BF16)
        for side in range(2):
            squares[2 * q + side, 0:64, :] = high[side * 64:side * 64 + 64]
            squares[2 * q + side, 64:128, :] = low[side * 64:side * 64 + 64]
    for t in range(2):
        kept = SENT - 192 - t * 32 if t == 1 else 32
        stage_low[...] = jnp.zeros_like(stage_low)
        for f in range(16):
            stage[f * 32:(f + 1) * 32, :] = gathered_ref[f, t * 32:(t + 1) * 32, :]
            stage_low[f * 32:f * 32 + kept, :] = gathered_ref[f, 192 + t * 32:192 + t * 32 + kept, :]
        start_ref[t * 128:(t + 1) * 128, :] = dot_nt(eye, stage[...]) + dot_nt(eye, stage_low[...])
    row = arrived_ref[704:720, :].astype(F32)[0:1, :]
    spot = lax.broadcasted_iota(jnp.int32, (1, 128), 1)
    for b in range(4):
        covers[b] = cover_ref[b]
        covers[4 + b] = jnp.sum(jnp.where(spot == b, row, 0.0)).astype(jnp.int32) - 8
        points[b] = point_ref[b]
        points_t[b] = flip_ref[b]
        weave_point(arrived_ref[192 + b * 128:320 + b * 128, :], points, points_t, 4 + b)


def opening_kernel(covers, bands, squares, points, points_t, start_ref, prior_cat, image,
                   mixer, vector_cat, vector_stack, vector, model, mixed, mixed_stack):
    first_tile = lax.axis_index("dish") * 2
    last, forms = False, None
    vector[...] = start_ref[...]
    build_mixer(covers, bands, squares, mixer)
    high, low = split(vector[...])
    vector_cat[:, 0:512] = high
    vector_cat[:, 512:1024] = high
    vector_cat[:, 1024:1536] = low
    for t in range(2):
        vector_stack[t, 0:128, :] = high[t * 128:(t + 1) * 128]
        vector_stack[t, 128:256, :] = low[t * 128:(t + 1) * 128]
    image[...] = jnp.dot(vector_cat[...], prior_cat[...], preferred_element_type=F32)

    @pl.loop(0, 8)
    def _(b):
        cover = covers[b] - first_tile

        @pl.when(jnp.logical_and(cover >= 0, cover < 2))
        def _():
            model[...] = jnp.dot(points[b], vector_stack[cover], preferred_element_type=F32)
            if last:
                forms[...] += square_form(b, mixer, model)
            else:
                apply_mixer(b, mixer, model, mixed)
                high, low = split(mixed[...])
                mixed_stack[0:128, :] = high
                mixed_stack[128:256, :] = low
                rows = pl.ds(pl.multiple_of(cover * 128, 128), 128)
                image[rows, :] += jnp.dot(points_t[b], mixed_stack[...], preferred_element_type=F32)


def krylov_kernel(covers, bands, squares, points, points_t, start_ref, scales_ref, prior_cat, factor_ref, first_ref,
                  moment_ref, scale,
                  mixer, vector_cat, vector_stack, vector, image, scale_rows, model, mixed, mixed_stack, forms):
    first_tile = lax.axis_index("dish") * 2
    vector[...] = start_ref[...]
    for f in range(16):
        scale_rows[f * 32:(f + 1) * 32, :] = scales_ref[f, 0:32, :]
    scale[...] = jnp.transpose(scale_rows[...])
    factor = factor_ref[0:1, 0:1]
    build_mixer(covers, bands, squares, mixer)

    def total(a, b):
        both = a * b
        both = both[:, 0:128] + both[:, 128:256] + (both[:, 256:384] + both[:, 384:512])
        return jnp.sum(both, axis=0, keepdims=True)

    forms[...] = jnp.zeros_like(forms)
    sums = [total(vector[...] * vector[...], 1.0 / scale[...])]
    for iteration in range(ITERS):
        last = iteration + 1 == ITERS
        if iteration == 0:
            image[...] = first_ref[...]
        else:
            high, low = split(vector[...])
            vector_cat[:, 0:512] = high
            vector_cat[:, 512:1024] = high
            vector_cat[:, 1024:1536] = low
            for t in range(2):
                vector_stack[t, 0:128, :] = high[t * 128:(t + 1) * 128]
                vector_stack[t, 128:256, :] = low[t * 128:(t + 1) * 128]
            image[...] = jnp.dot(vector_cat[...], prior_cat[...], preferred_element_type=F32)

            @pl.loop(0, 8)
            def _(b):
                cover = covers[b] - first_tile

                @pl.when(jnp.logical_and(cover >= 0, cover < 2))
                def _():
                    model[...] = jnp.dot(points[b], vector_stack[cover], preferred_element_type=F32)
                    if last:
                        forms[...] += square_form(b, mixer, model)
                    else:
                        apply_mixer(b, mixer, model, mixed)
                        high, low = split(mixed[...])
                        mixed_stack[0:128, :] = high
                        mixed_stack[128:256, :] = low
                        rows = pl.ds(pl.multiple_of(cover * 128, 128), 128)
                        image[rows, :] += jnp.dot(points_t[b], mixed_stack[...], preferred_element_type=F32)

        result = image[...]
        found = total(vector[...], result)
        if last:
            found = found + jnp.sum(forms[...], axis=0, keepdims=True)
        sums.append(found)
        if not last:
            following = scale[...] * result * factor
            vector[...] = following
            sums.append(total(following, result))
    sums = jnp.concatenate(sums, axis=0)
    for i in range(32):
        moment_ref[i] = sums


def steps_of(moments_ref, factor):
    sums = moments_ref[0]
    for i in range(1, 32):
        sums = sums + moments_ref[i]
    sums = jnp.broadcast_to(jnp.sum(sums, axis=1, keepdims=True), (8, 128))
    mu = [sums[n:n + 1, :] for n in range(8)]
    one = jnp.ones((1, 128), F32)
    norm = [one / jnp.sqrt(mu[2 * i + 1]) for i in range(4)]
    system = [[mu[i + j + 1] * norm[i] * norm[j] for j in range(4)] for i in range(4)]
    target = [(mu[0] if i == 0 else mu[i] * factor) * norm[i] for i in range(4)]
    lower = [[None] * 4 for _ in range(4)]
    inverse, pivot, forward = [None] * 4, [None] * 4, [None] * 4
    alphas, energies = [], []
    lead, sound = one, one > 0.0
    for i in range(4):
        for j in range(i):
            value = system[i][j]
            for m in range(j):
                value = value - lower[i][m] * lower[j][m] * pivot[m]
            lower[i][j] = value * inverse[j]
        value, aim = system[i][i], target[i]
        for m in range(i):
            value = value - lower[i][m] * lower[i][m] * pivot[m]
            aim = aim - lower[i][m] * forward[m]
        sound = jnp.logical_and(sound, value > 1e-6)
        pivot[i] = value
        inverse[i] = jnp.where(sound, one / value, 0.0)
        forward[i] = aim
        scaled = jnp.where(sound, lead / norm[i], one)
        alpha = aim * inverse[i] / scaled
        alphas.append(alpha)
        energies.append(alpha * scaled * scaled * pivot[i])
        sound = jnp.logical_and(sound, energies[i] > 0.0)
        lead = jnp.where(sound, -lead * alpha / factor, one)
        if i > 0:
            energies[i - 1] = jnp.where(sound, energies[i] / energies[i - 1], 0.0)
    return alphas, energies[:3]


def replay_kernel(covers, moments_ref, factor_ref, bands, squares, points, points_t, prior_cat, start_ref, scale,
                  right_ref, estimate_ref, residual_ref,
                  mixer, vector_cat, vector, carried, image, estimate, removed, model, mixed):
    first_tile = lax.axis_index("dish") * 2
    mine = choose_own()
    alphas, betas = steps_of(moments_ref, factor_ref[0:1, :])
    alphas = [value[0:1, 0:1] for value in alphas]
    betas = [value[0:1, 0:1] for value in betas]
    build_mixer(covers, bands, squares, mixer)
    vector[...] = start_ref[...]
    carried[...] = start_ref[...]
    for iteration in range(ITERS):
        high, low = split(vector[...])
        vector_cat[:, 0:512] = high
        vector_cat[:, 512:1024] = high
        vector_cat[:, 1024:1536] = low
        image[...] = jnp.dot(vector_cat[...], prior_cat[...], preferred_element_type=F32)

        @pl.loop(0, 8)
        def _(b):
            cover = covers[b] - first_tile

            @pl.when(jnp.logical_and(cover >= 0, cover < 2))
            def _():
                rows = pl.ds(pl.multiple_of(cover * 128, 128), 128)
                made = jnp.dot(points[b, :, 0:128], vector_cat[rows, 0:512], preferred_element_type=F32)
                model[...] = made.astype(BF16).astype(F32)
                apply_mixer(b, mixer, model, mixed)
                half = mixed[...].astype(BF16)
                image[rows, :] += jnp.dot(points_t[b, :, 0:128], half, preferred_element_type=F32)

        alpha = alphas[iteration]
        result = alpha * image[...]
        if iteration == 0:
            estimate[...] = alpha * vector[...]
            removed[...] = result
        else:
            estimate[...] = estimate[...] + alpha * vector[...]
            removed[...] = removed[...] + result
        if iteration + 1 < ITERS:
            moved = carried[...] - scale[...] * result
            carried[...] = moved
            vector[...] = moved + betas[iteration] * vector[...]
    high, low = split(estimate[...])
    estimate_ref[...] = dot_nt(mine, high) + dot_nt(mine, low)
    high, low = split(removed[...])
    residual_ref[...] = right_ref[...] - (dot_nt(mine, high) + dot_nt(mine, low))


def shape(dims, kind):
    return jax.ShapeDtypeStruct(dims, kind)


def body(time_data, pointing, coverage, noise_inv, gains, prior_inv, precond):
    spread = lax.all_gather(jnp.concatenate([precond, precond]), "freq", axis=0)
    packed = pl.pallas_call(
        prepare_kernel,
        out_shape=shape((592, 128), BF16),
        in_specs=[VMEM, VMEM, VMEM],
        out_specs=VMEM,
        scratch_shapes=[pltpu.VMEM((512, 128), F32)],
        compiler_params=pltpu.CompilerParams(vmem_limit_bytes=10 * 1024 * 1024),
        name="prepare",
    )(time_data, noise_inv, jnp.swapaxes(gains, 1, 2))
    over_dish = lax.all_gather(packed, "dish", axis=0)
    own, square, ahead = pl.pallas_call(
        project_kernel,
        out_shape=(shape((64, 128), F32), shape((64, 128), BF16), shape((720, 128), BF16)),
        in_specs=[SMEM, VMEM, VMEM],
        out_specs=(VMEM, VMEM, VMEM),
        compiler_params=pltpu.CompilerParams(vmem_limit_bytes=6 * 1024 * 1024),
        name="project",
    )(coverage, over_dish, pointing)
    count = lax.axis_size("tm")
    arrived = lax.ppermute(ahead, "tm", [(i, (i + 1) % count) for i in range(count)])
    prior_cat, bands, points, points_t, factor = pl.pallas_call(
        setup_kernel,
        out_shape=(shape((1536, 512), BF16), shape((DIAGS * 128, 128), BF16), shape((4, 128, 256), BF16),
                   shape((4, 128, 256), BF16), shape((8, 128), F32)),
        in_specs=[VMEM] * 3,
        out_specs=(VMEM,) * 5,
        cost_estimate=pl.CostEstimate(flops=200_000_000, bytes_accessed=6_000_000, transcendentals=0),
        compiler_params=pltpu.CompilerParams(vmem_limit_bytes=14 * 1024 * 1024),
        name="setup",
    )(over_dish, prior_inv, pointing)
    right, packed = pl.pallas_call(
        start_kernel,
        out_shape=(shape((32, 256), F32), shape((SENT, 128), BF16)),
        in_specs=[VMEM] * 4,
        out_specs=(VMEM, VMEM),
        compiler_params=pltpu.CompilerParams(vmem_limit_bytes=4 * 1024 * 1024),
        name="start",
    )(own, square, arrived, precond)
    over_freq = lax.all_gather(packed, "freq", axis=0)
    whole = (256, 512)
    covers, squares, points, points_t, first = pl.pallas_call(
        assemble_kernel,
        out_shape=(shape((8,), jnp.int32), shape((8, 128, 512), BF16),
                   shape((8, 128, 256), BF16), shape((8, 128, 256), BF16), shape(whole, F32)),
        in_specs=[SMEM] + [VMEM] * 4,
        out_specs=(SMEM,) + (VMEM,) * 4,
        scratch_shapes=[pltpu.VMEM((512, 128), BF16), pltpu.VMEM((512, 128), BF16)],
        cost_estimate=pl.CostEstimate(flops=300_000_000, bytes_accessed=4_000_000, transcendentals=0),
        compiler_params=pltpu.CompilerParams(vmem_limit_bytes=12 * 1024 * 1024),
        name="assemble",
    )(coverage, over_freq, points, points_t, arrived)
    opened = pl.pallas_call(
        opening_kernel,
        out_shape=shape(whole, F32),
        in_specs=[SMEM] + [VMEM] * 6,
        out_specs=VMEM,
        scratch_shapes=[
            pltpu.VMEM((8, 4, DIAGS * 128, 128), F32),
            pltpu.VMEM((256, 1536), BF16),
            pltpu.VMEM((2, 256, 512), BF16),
            pltpu.VMEM(whole, F32),
            pltpu.VMEM((128, 512), F32),
            pltpu.VMEM((128, 512), F32),
            pltpu.VMEM(whole, BF16),
        ],
        cost_estimate=pl.CostEstimate(flops=2_000_000_000, bytes_accessed=10_000_000, transcendentals=0),
        compiler_params=pltpu.CompilerParams(vmem_limit_bytes=50 * 1024 * 1024),
        name="opening",
    )(covers, bands, squares, points, points_t, first, prior_cat)
    moments, scale = pl.pallas_call(
        krylov_kernel,
        out_shape=(shape((32, 8, 128), F32), shape(whole, F32)),
        in_specs=[SMEM] + [VMEM] * 9,
        out_specs=(VMEM, VMEM),
        scratch_shapes=[
            pltpu.VMEM((8, 4, DIAGS * 128, 128), F32),
            pltpu.VMEM((256, 1536), BF16),
            pltpu.VMEM((2, 256, 512), BF16),
            pltpu.VMEM(whole, F32),
            pltpu.VMEM(whole, F32),
            pltpu.VMEM((512, 256), F32),
            pltpu.VMEM((128, 512), F32),
            pltpu.VMEM((128, 512), F32),
            pltpu.VMEM(whole, BF16),
            pltpu.VMEM((8, 128), F32),
        ],
        compiler_params=pltpu.CompilerParams(vmem_limit_bytes=50 * 1024 * 1024),
        name="krylov",
    )(covers, bands, squares, points, points_t, first, spread, prior_cat, factor, opened)
    shared = lax.all_to_all(moments, ("tm", "dish"), split_axis=0, concat_axis=0)
    return tuple(pl.pallas_call(
        replay_kernel,
        out_shape=(shape((32, 256), F32), shape((32, 256), F32)),
        in_specs=[SMEM] + [VMEM] * 10,
        out_specs=(VMEM, VMEM),
        scratch_shapes=[
            pltpu.VMEM((8, 4, DIAGS * 128, 128), F32),
            pltpu.VMEM((256, 1536), BF16),
            pltpu.VMEM(whole, F32),
            pltpu.VMEM(whole, F32),
            pltpu.VMEM(whole, F32),
            pltpu.VMEM(whole, F32),
            pltpu.VMEM(whole, F32),
            pltpu.VMEM((128, 512), F32),
            pltpu.VMEM((128, 512), F32),
        ],
        compiler_params=pltpu.CompilerParams(vmem_limit_bytes=50 * 1024 * 1024),
        name="replay",
    )(covers, shared, factor, bands, squares, points, points_t, prior_cat, first, scale, right))


def solution(mesh):
    return jax.shard_map(
        body,
        mesh=mesh,
        in_specs=(
            P("dish", "freq", "tm"),
            P("tm", None, None),
            P("tm"),
            P("dish", None, None),
            P("dish", "freq", "tm"),
            P(),
            P("freq", ("tm", "dish")),
        ),
        out_specs=(P("freq", ("tm", "dish")), P("freq", ("tm", "dish"))),
        check_vma=False,
    )
```
